512 devices in a mesh: seq: 128 (over z, y_lo, x), doc: 4 (over y_hi, core).
Axes of the slice: x: 4, y: 8 (y_hi: 2, y_lo: 4; y = y_hi * 4 + y_lo), z: 8, core: 2. Of those that a mesh axis runs over, the one named last changes fastest.
Arguments:
- inputs: bfloat16 [65536, 1024], P('seq', 'doc'), may hold values from -4 to 4
- queries: bfloat16 [65536, 1024], P('seq', 'doc'), may hold values from -128 to 128
- keys_values: bfloat16 [2, 65536, 1024], P(None, 'seq', 'doc'), may hold values from -10 to 10
- slot_weight: bfloat16 [1024, 4096], P(None, 'doc'), may hold values from -3 to 3
- slot_gain: float32 [2, 1024], P(None, 'doc'), may hold values from 0.1 to 1.9
- slot_bias: float32 [2, 1024], P(None, 'doc'), may hold values from -3 to 3
- bounds: int32 [2, 65536], P(None, 'seq'), may hold values from 0 to 65536, as said below
Outputs:
- attended: bfloat16 [65536, 1024], P('seq', 'doc')
The draws below stay inside these ranges and needn't reach their ends.
Inputs may be any that keep to these rules, and one draw needn't show every extreme that they name: The sequence holds exactly 2 documents in order, the first starting at 0 and each of 16384 tokens or more: bounds[0, i] <= i < bounds[1, i], and every token of a document has the same pair.
All inputs are finite; a program needn't handle non-finite values.
Results may differ from the reference program's by a relative error of at most 0.0045.
Values may be sent and summed in bfloat16 or wider, within the bound.
No kernel may reach another device: no remote copies, remote signals or barrier semaphores. Data moves between devices by JAX's collectives and lax.ppermute only.
A program may use at most 64 MiB of HBM per device.

```python
import math
import jax
import jax.numpy as jnp
from jax import lax

H = 16
DH = 64
R = 256
W = 128
DOCS = 2
D = 1024
TOKENS = 65536


def draw_inputs(key, part):
    drawn = jax.random.truncated_normal(jax.random.fold_in(key, 21), -4.0, 4.0, (TOKENS, D))
    return drawn.astype(jnp.bfloat16)


def draw_slot_weight(key, part):
    drawn = 0.0625 * jax.random.truncated_normal(jax.random.fold_in(key, 22), -4.0, 4.0, (D, H * R))
    return drawn.astype(jnp.bfloat16)


def draw_keys_values(key, part):
    drawn = jax.random.truncated_normal(jax.random.fold_in(key, 23), -4.0, 4.0, (2, TOKENS, D))
    return drawn.astype(jnp.bfloat16)


def draw_queries(key, part):
    drawn = 1.2 * jax.random.truncated_normal(jax.random.fold_in(key, 24), -4.0, 4.0, (TOKENS, D))
    return drawn.astype(jnp.bfloat16)


def draw_bounds(key, part):
    places = jnp.arange(TOKENS, dtype=jnp.int32)
    split_at = jax.random.randint(jax.random.fold_in(key, 31), (), TOKENS // 4, TOKENS - TOKENS // 4 + 1)
    later = places >= split_at
    starts = jnp.where(later, split_at, 0)
    doc_end = jnp.where(later, TOKENS, split_at)
    return jnp.stack([starts, doc_end]).astype(jnp.int32)


def steps_of(stream_key, dims, cuts, low, top_value):
    def one(position, shards_of):
        steps = jax.random.uniform(jax.random.fold_in(jax.random.fold_in(stream_key, 6), position), (shards_of,), jnp.float32, low / len(cuts), top_value / len(cuts))
        return jnp.repeat(jnp.exp(steps), dims[position] // shards_of).reshape((-1,) + (1,) * (len(dims) - position - 1))

    level = one(*cuts[0])
    for cut in cuts[1:]:
        level = level * one(*cut)
    return level


def normal_values(key, shape, width, bound, shards=(), held_as=jnp.bfloat16):
    values = width * jax.random.normal(key, shape, jnp.float32)
    if shards:
        values = values * steps_of(key, shape, shards, -0.22, 0.18)
    return jnp.clip(values, -bound, bound).astype(held_as)


def setup_inputs(seed: int = 0) -> dict:
    key_of = jax.random.split(jax.random.key(seed), 8)
    inputs = draw_inputs(jax.random.fold_in(key_of[7], 71), 0)
    queries = draw_queries(jax.random.fold_in(key_of[7], 71), 0)
    keys_values = draw_keys_values(jax.random.fold_in(key_of[7], 71), 0)
    slot_weight = draw_slot_weight(jax.random.fold_in(key_of[7], 71), 0)
    slot_gain = jnp.clip(1.0 + 0.18 * jax.random.normal(key_of[4], (2, D), jnp.float32), 0.1, 1.9)
    slot_bias = normal_values(key_of[5], (2, D), 0.5, 3.0, ((1, 4),), jnp.float32)
    bounds = draw_bounds(jax.random.fold_in(key_of[7], 71), 0)
    return dict(inputs=inputs, queries=queries, keys_values=keys_values, slot_weight=slot_weight, slot_gain=slot_gain, slot_bias=slot_bias, bounds=bounds)


epsilon = 1e-05

def normalize(numerator, gain, bias):
    mean_val = lax.optimization_barrier(jnp.mean(numerator, axis=-1, keepdims=True))
    centred = numerator - mean_val
    variance = lax.optimization_barrier(jnp.mean(centred * centred, axis=-1, keepdims=True))
    return centred * lax.rsqrt(variance + epsilon) * gain + bias

def attend(query_block, window, lower, upper, first_pos, slot_keys, slot_values):
    q_len = query_block.shape[0]
    k_len = window.shape[1]
    second = (lower > 0)[None, :, None]
    near_scores = jnp.einsum('qhe,khe->hqk', query_block, window[0]) * 0.125
    far_all = jnp.einsum('qhe,ghre->ghqr', query_block, slot_keys) * 0.125
    far_scores = jnp.where(second, far_all[1], far_all[0])
    query_pos = first_pos + jnp.arange(q_len, dtype=jnp.int32)
    key_pos = first_pos - W + jnp.arange(k_len, dtype=jnp.int32)
    offset = key_pos[None, :] - query_pos[:, None]
    allowed = (jnp.abs(offset) <= W) & (key_pos[None, :] >= lower[:, None]) & (key_pos[None, :] < upper[:, None])
    near_scores = jnp.where(allowed[None], near_scores, -jnp.inf)
    row_top = jnp.maximum(lax.optimization_barrier(jnp.max(near_scores, axis=-1)), lax.optimization_barrier(jnp.max(far_scores, axis=-1)))
    near_weight = jnp.exp(near_scores - row_top[..., None])
    far_weight = jnp.exp(far_scores - row_top[..., None])
    row_total = lax.optimization_barrier(jnp.sum(near_weight, axis=-1)) + lax.optimization_barrier(jnp.sum(far_weight, axis=-1))
    near_b = lax.optimization_barrier(near_weight.astype(jnp.bfloat16)).astype(jnp.float32)
    far_b = lax.optimization_barrier(far_weight.astype(jnp.bfloat16)).astype(jnp.float32)
    zero_val = jnp.zeros((), jnp.float32)
    result = jnp.einsum('hqk,khe->qhe', near_b, window[1])
    result = result + jnp.einsum('hqr,hre->qhe', jnp.where(second, zero_val, far_b), slot_values[0])
    result = result + jnp.einsum('hqr,hre->qhe', jnp.where(second, far_b, zero_val), slot_values[1])
    result = result / jnp.transpose(row_total)[:, :, None]
    return result.reshape(q_len, H * DH).astype(jnp.bfloat16)

def reference(inputs, queries, keys_values, slot_weight, slot_gain, slot_bias, bounds):
    blk_len = math.gcd(TOKENS, 4096)
    blk_count = TOKENS // blk_len
    blocks = jnp.arange(blk_count, dtype=jnp.int32)
    doc_ids = (bounds[0] > 0).astype(jnp.int32)

    def block_logits(block_at):
        feature_rows = lax.dynamic_slice_in_dim(inputs, block_at * blk_len, blk_len, 0)
        return jnp.dot(feature_rows, slot_weight, preferred_element_type=jnp.float32)

    def block_docs(block_at):
        return lax.dynamic_slice_in_dim(doc_ids, block_at * blk_len, blk_len, 0)

    def top_step(running, block_at):
        logits = block_logits(block_at)
        owner = block_docs(block_at)
        first = lax.optimization_barrier(jnp.max(jnp.where((owner == 0)[:, None], logits, -jnp.inf), axis=0))
        other = lax.optimization_barrier(jnp.max(jnp.where((owner == 1)[:, None], logits, -jnp.inf), axis=0))
        return (jnp.maximum(running, jnp.stack([first, other])), None)
    slot_top, _ = lax.scan(top_step, jnp.full((DOCS, H * R), -jnp.inf, jnp.float32), blocks)

    def sum_step(running, block_at):
        owner = block_docs(block_at)
        top_rows = jnp.where((owner == 1)[:, None], slot_top[1][None, :], slot_top[0][None, :])
        proj = lax.optimization_barrier(jnp.exp(block_logits(block_at) - top_rows).astype(jnp.bfloat16))
        proj = proj.astype(jnp.float32).reshape(blk_len, H, R)
        picks = jnp.stack([owner == 0, owner == 1]).astype(jnp.float32)
        kv_pair = lax.dynamic_slice_in_dim(keys_values, block_at * blk_len, blk_len, 1).astype(jnp.float32)
        kv_pair = kv_pair.reshape(2, blk_len, H, DH)
        return (running + jnp.einsum('gt,thr,stha->ghrsa', picks, proj, kv_pair), None)
    numerator, _ = lax.scan(sum_step, jnp.zeros((DOCS, H, R, 2, DH), jnp.float32), blocks)
    gain = jnp.transpose(slot_gain.reshape(2, H, DH), (1, 0, 2))[None, :, None]
    bias = jnp.transpose(slot_bias.reshape(2, H, DH), (1, 0, 2))[None, :, None]
    slot_table = normalize(numerator, gain, bias).astype(jnp.bfloat16).astype(jnp.float32)
    slot_keys = slot_table[:, :, :, 0]
    slot_values = slot_table[:, :, :, 1]
    q_len = math.gcd(TOKENS, 512)
    padded = jnp.pad(keys_values, ((0, 0), (W, W), (0, 0)))

    def one_block(block_at):
        start_at = block_at * q_len
        query_block = lax.dynamic_slice_in_dim(queries, start_at, q_len, 0).astype(jnp.float32).reshape(q_len, H, DH)
        window = lax.dynamic_slice_in_dim(padded, start_at, q_len + 2 * W, 1).astype(jnp.float32)
        window = window.reshape(2, q_len + 2 * W, H, DH)
        lower = lax.dynamic_slice_in_dim(bounds[0], start_at, q_len, 0)
        upper = lax.dynamic_slice_in_dim(bounds[1], start_at, q_len, 0)
        return attend(query_block, window, lower, upper, start_at, slot_keys, slot_values)
    outputs = lax.map(one_block, jnp.arange(TOKENS // q_len, dtype=jnp.int32))
    return outputs.reshape(TOKENS, H * DH)
```

```python
import functools

import jax
import jax.numpy as jnp
from jax import lax
from jax.experimental import pallas as pl
from jax.experimental.pallas import tpu as pltpu
from jax.sharding import Mesh
from jax.sharding import PartitionSpec as P

DH = 64
R = 256
W = 128
HEADS = 4
LANES = 128
ROWS = 8
SEQ = ("z", "yl", "x")
DOC = ("yh", "c")
EPS = 1e-05
LOW = -1e30
SWAP = [(0, 1), (1, 0)]

f32 = jnp.float32
bf16 = jnp.bfloat16
VMEM = pl.BlockSpec(memory_space=pltpu.VMEM)
SMEM = pl.BlockSpec(memory_space=pltpu.SMEM)


def call(kernel, out_shape, n_in, vmem_mib, flops, nbytes, exps=0):
    single = not isinstance(out_shape, (list, tuple))
    return pl.pallas_call(
        kernel,
        out_shape=out_shape,
        in_specs=[SMEM] + [VMEM] * n_in,
        out_specs=VMEM if single else [VMEM] * len(out_shape),
        compiler_params=pltpu.CompilerParams(vmem_limit_bytes=vmem_mib << 20),
        cost_estimate=pl.CostEstimate(flops=flops, bytes_accessed=nbytes, transcendentals=exps),
    )


def dot_nt(a, b):
    return lax.dot_general(a, b, (((1,), (1,)), ((), ())), preferred_element_type=f32)


def lanes_of(shape):
    return lax.broadcasted_iota(jnp.int32, shape, len(shape) - 1)


def prep_kernel(scal, q_ref, kv_ref, q2_ref, kvh_ref):
    tokens = q_ref.shape[0]
    local = scal[0]
    second = lax.broadcasted_iota(jnp.int32, (tokens, LANES), 0) >= local
    left = lanes_of((tokens, LANES)) < DH
    for pair in range(HEADS // 2):
        cols = slice(pair * LANES, (pair + 1) * LANES)
        query = q_ref[:, cols].astype(f32) * 0.125
        keys = kv_ref[0, :, cols].astype(f32)
        values = kv_ref[1, :, cols].astype(f32)
        query_r = pltpu.roll(query, DH, 1)
        keys_r = pltpu.roll(keys, DH, 1)
        values_r = pltpu.roll(values, DH, 1)
        for half in range(2):
            h = 2 * pair + half
            both = jnp.where(left, query, query_r) if half == 0 else jnp.where(left, query_r, query)
            q2_ref[h] = jnp.where(left == second, 0.0, both).astype(bf16)
            joined = jnp.where(left, keys, values_r) if half == 0 else jnp.where(left, keys_r, values)
            kvh_ref[h, :, :LANES] = jnp.where(second, 0.0, joined).astype(bf16)
            kvh_ref[h, :, LANES:] = jnp.where(second, joined, 0.0).astype(bf16)


def near_kernel(scal, q_ref, kv_ref, before_ref, after_ref, o_ref, stat_ref):
    tokens = q_ref.shape[0]
    local, base, total = scal[0], scal[1], scal[2]
    blocks = tokens // W
    span = 3 * W
    row = lax.broadcasted_iota(jnp.int32, (W, span), 0)
    col = lax.broadcasted_iota(jnp.int32, (W, span), 1)
    band = (col >= row) & (col - row <= 2 * W)
    left = lanes_of((W, LANES)) < DH
    lane = lanes_of((W, LANES))

    def piece(s, at, cols):
        if at < 0:
            return before_ref[s, :, cols]
        if at >= blocks:
            return after_ref[s, :, cols]
        return kv_ref[s, at * W : (at + 1) * W, cols]

    for b in range(blocks):
        query_pos = row + b * W
        key_pos = col + (b - 1) * W
        allowed = (
            band
            & ((query_pos >= local) == (key_pos >= local))
            & (key_pos + base >= 0)
            & (key_pos + base < total)
        )
        stats = jnp.zeros((W, LANES), f32)
        for pair in range(HEADS // 2):
            cols = slice(pair * LANES, (pair + 1) * LANES)
            query = q_ref[b * W : (b + 1) * W, cols].astype(f32) * 0.125
            keys = jnp.concatenate([piece(0, b + i, cols) for i in (-1, 0, 1)], axis=0)
            values = jnp.concatenate([piece(1, b + i, cols) for i in (-1, 0, 1)], axis=0)
            outs = []
            for half in range(2):
                h = 2 * pair + half
                mine = jnp.where(left == (half == 0), query, 0.0).astype(bf16)
                scores = jnp.where(allowed, dot_nt(mine, keys), LOW)
                top = jnp.max(scores, axis=1, keepdims=True)
                weight = jnp.exp(scores - top)
                total_w = jnp.sum(weight, axis=1, keepdims=True)
                outs.append(jnp.dot(weight.astype(bf16), values, preferred_element_type=f32))
                stats = jnp.where(lane == h, top, stats)
                stats = jnp.where(lane == HEADS + h, total_w, stats)
            o_ref[b * W : (b + 1) * W, cols] = jnp.where(left, outs[0], outs[1])
        stat_ref[b * W : (b + 1) * W, :] = stats


def pieces_of(top):
    a = top.astype(bf16).astype(f32)
    b = (top - a).astype(bf16).astype(f32)
    return a, b, top - a - b


def project_kernel(scal, x0, x1, x2, x3, wt_ref, kvh_ref, out_ref):
    tokens = x0.shape[0]
    local = scal[0]
    second = lax.broadcasted_iota(jnp.int32, (R, tokens), 1) >= local
    mixed = jnp.logical_and(local > 0, local < tokens)
    lane = lanes_of((R, LANES))
    at_a = lane == 0
    at_b = lane == DH
    left = lane < DH
    for h in range(HEADS):
        rows = slice(h * R, (h + 1) * R)
        logits = dot_nt(wt_ref[scal[3], rows, :], x0[...])
        logits += dot_nt(wt_ref[scal[4], rows, :], x1[...])
        logits += dot_nt(wt_ref[scal[5], rows, :], x2[...])
        logits += dot_nt(wt_ref[scal[6], rows, :], x3[...])
        top0 = jnp.maximum(jnp.max(jnp.where(second, LOW, logits), axis=1, keepdims=True), LOW)
        top1 = jnp.maximum(jnp.max(jnp.where(second, logits, LOW), axis=1, keepdims=True), LOW)
        a0, b0, c0 = pieces_of(top0)
        a1, b1, c1 = pieces_of(top1)
        proj = jnp.exp(logits - jnp.where(second, a1 + b1, a0 + b0)).astype(bf16)
        sums = jnp.dot(proj, kvh_ref[h], preferred_element_type=f32)
        n0 = sums[:, :LANES]
        n1 = sums[:, LANES:]
        n0 = n0 - jnp.where(left, n0[:, 0:1], n0[:, DH : DH + 1])
        n1 = n1 - jnp.where(left, n1[:, 0:1], n1[:, DH : DH + 1])
        late = local <= 0
        a_p, b_p, c_p = (jnp.where(late, u1, u0) for u0, u1 in ((a0, a1), (b0, b1), (c0, c1)))
        body = jnp.where(mixed, n0, n0 + n1)
        hi = body.astype(bf16).astype(f32)
        rest = jnp.where(mixed, n1, body - hi)
        hi = jnp.where(at_a, a_p, jnp.where(at_b, b_p, hi))
        rest = jnp.where(
            at_a,
            jnp.where(mixed, a1, c_p),
            jnp.where(at_b, jnp.where(mixed, b1, jnp.zeros_like(b1)), rest),
        )
        parts = R // ROWS
        packed = jnp.concatenate(
            [hi.reshape(parts, ROWS, LANES), rest.reshape(parts, ROWS, LANES)], axis=1
        )
        out_ref[h * parts : (h + 1) * parts] = packed.astype(bf16)


def combine_kernel(scal, in_ref, gain_ref, bias_ref, out_ref):
    senders = in_ref.shape[0]
    split, tokens = scal[0], scal[1]
    edge = split // tokens
    has_edge = lax.rem(split, tokens) != 0
    shape = (senders, ROWS, LANES)
    j = lax.broadcasted_iota(jnp.int32, shape, 0)
    is_edge = jnp.logical_and(j == edge, has_edge)
    late = j * tokens >= split
    first = in_ref[:, :ROWS, :].astype(f32)
    other = in_ref[:, ROWS:, :].astype(f32)
    top = first[:, :, 0:1] + first[:, :, DH : DH + 1]
    top = jnp.broadcast_to(top, shape)
    fine = jnp.where(is_edge, 0.0, jnp.broadcast_to(other[:, :, 0:1], shape))
    value = jnp.where(is_edge, first, first + other)
    extra = in_ref[edge % senders].astype(f32)[ROWS:]
    extra_top = jnp.broadcast_to(extra[:, 0:1] + extra[:, DH : DH + 1], (ROWS, LANES))
    extra_top = jnp.where(has_edge, extra_top, LOW)
    top0 = jnp.max(jnp.where(late, LOW, top), axis=0)
    full0 = jnp.max(jnp.where(late, LOW, top + fine), axis=0)
    top1 = jnp.maximum(jnp.max(jnp.where(late, top, LOW), axis=0), extra_top)
    full1 = jnp.maximum(jnp.max(jnp.where(late, top + fine, LOW), axis=0), extra_top)
    weight = jnp.exp(top - jnp.where(late, top1[None], top0[None]))
    value = value * weight
    n0 = jnp.sum(jnp.where(late, 0.0, value), axis=0)
    n1 = jnp.sum(jnp.where(late, value, 0.0), axis=0)
    n1 = n1 + jnp.where(has_edge, extra * jnp.exp(extra_top - top1), 0.0)
    lane = lanes_of((ROWS, LANES))
    left = lane < DH
    used = jnp.logical_and(lane != 0, lane != DH)
    gain = gain_ref[...]
    bias = bias_ref[...]

    def halves(v):
        a = jnp.sum(jnp.where(left, v, 0.0), axis=1, keepdims=True)
        b = jnp.sum(jnp.where(left, 0.0, v), axis=1, keepdims=True)
        return jnp.where(left, a, b) * (1.0 / DH)

    def norm(n, top_v, full_v):
        n = jnp.where(used, n, 0.0)
        centred = n - halves(n)
        variance = halves(centred * centred)
        scale = jnp.exp(2.0 * (full_v - top_v))
        return centred * lax.rsqrt(variance + EPS * scale) * gain + bias

    t0 = norm(n0, top0, full0)
    t1 = norm(n1, top1, full1)
    keys = jnp.where(left, t0, pltpu.roll(t1, DH, 1))
    values = jnp.where(left, pltpu.roll(t0, DH, 1), t1)
    chunk = jnp.concatenate([keys, values], axis=0)[None]
    out_ref[...] = jnp.broadcast_to(chunk, out_ref.shape).astype(bf16)


def far_kernel(scal, q2_ref, tab_ref, o_ref, stat_ref, out_ref):
    tokens = o_ref.shape[0]
    local = scal[0]
    lane = lanes_of((tokens, LANES))
    left = lane < DH
    second = lax.broadcasted_iota(jnp.int32, (tokens, LANES), 0) >= local
    parts = R // ROWS
    stats = stat_ref[...]
    for pair in range(HEADS // 2):
        cols = slice(pair * LANES, (pair + 1) * LANES)
        near = o_ref[:, cols]
        outs = []
        for half in range(2):
            h = 2 * pair + half
            table = tab_ref[h * parts : (h + 1) * parts].astype(f32)
            keys = table[:, :ROWS].reshape(R, LANES).astype(bf16)
            values = table[:, ROWS:].reshape(R, LANES).astype(bf16)
            scores = dot_nt(q2_ref[h], keys)
            near_top = stats[:, h : h + 1]
            near_total = stats[:, HEADS + h : HEADS + h + 1]
            top = jnp.maximum(jnp.max(scores, axis=1, keepdims=True), near_top)
            weight = jnp.exp(scores - top)
            scale = jnp.exp(near_top - top)
            total = jnp.sum(weight, axis=1, keepdims=True) + near_total * scale
            far = jnp.dot(weight.astype(bf16), values, preferred_element_type=f32)
            swap = second if half == 0 else jnp.logical_not(second)
            far = jnp.where(swap, pltpu.roll(far, DH, 1), far)
            outs.append((near * scale + far) / total)
        out_ref[:, cols] = jnp.where(left, outs[0], outs[1]).astype(bf16)


def on_device(inputs, queries, keys_values, slot_weight, slot_gain, slot_bias, bounds):
    tokens, width = inputs.shape
    shards = lax.axis_size(SEQ)
    shard = lax.axis_index(SEQ)
    split = jnp.where(bounds[0, 0] > 0, bounds[0, 0], bounds[1, 0])
    base = shard * tokens
    yh, c = lax.axis_index("yh"), lax.axis_index("c")
    scal = jnp.stack(
        [
            split - base,
            base,
            jnp.int32(shards * tokens),
            yh * 2 + c,
            yh * 2 + 1 - c,
            (1 - yh) * 2 + c,
            (1 - yh) * 2 + 1 - c,
        ]
    ).astype(jnp.int32)
    scal2 = jnp.stack([split, jnp.int32(tokens)]).astype(jnp.int32)

    x2 = lax.ppermute(inputs, "yh", SWAP)
    x1 = lax.ppermute(inputs, "c", SWAP)
    x3 = lax.ppermute(x2, "c", SWAP)
    up = [(i, i + 1) for i in range(shards - 1)]
    down = [(j, i) for i, j in up]
    before = lax.ppermute(keys_values[:, tokens - W :], SEQ, up)
    after = lax.ppermute(keys_values[:, :W], SEQ, down)

    weight_t = jnp.swapaxes(slot_weight.reshape(4, width, HEADS * R), 1, 2)
    q2, kvh = call(
        prep_kernel,
        [
            jax.ShapeDtypeStruct((HEADS, tokens, LANES), bf16),
            jax.ShapeDtypeStruct((HEADS, tokens, 2 * LANES), bf16),
        ],
        2, 16, 0, 3 << 20,
    )(scal, queries, keys_values)

    sent = call(
        project_kernel,
        jax.ShapeDtypeStruct((shards, 2 * ROWS, LANES), bf16),
        6, 24, 2 * tokens * HEADS * R * (4 * width + 2 * LANES), 5 << 20, tokens * HEADS * R,
    )(scal, inputs, x1, x2, x3, weight_t, kvh)
    arrived = lax.all_to_all(sent, SEQ, 0, 0, tiled=True)

    near, stats = call(
        near_kernel,
        [
            jax.ShapeDtypeStruct((tokens, HEADS * DH), f32),
            jax.ShapeDtypeStruct((tokens, LANES), f32),
        ],
        4, 16, 4 * tokens * 3 * W * HEADS * LANES, 2 << 20, tokens * 3 * W * HEADS,
    )(scal, queries, keys_values, before, after)

    head = shard * ROWS // R
    gain = lax.dynamic_slice_in_dim(slot_gain, head * DH, DH, 1).reshape(1, 2 * DH)
    bias = lax.dynamic_slice_in_dim(slot_bias, head * DH, DH, 1).reshape(1, 2 * DH)
    chunk = call(
        combine_kernel,
        jax.ShapeDtypeStruct((shards, 2 * ROWS, LANES), bf16),
        3, 16, 0, 1 << 20, 1 << 17,
    )(scal2, arrived, gain, bias)
    table = lax.all_to_all(chunk, SEQ, 0, 0, tiled=True)

    return call(
        far_kernel,
        jax.ShapeDtypeStruct((tokens, HEADS * DH), bf16),
        4, 24, 4 * tokens * R * HEADS * LANES, 2 << 20, tokens * R * HEADS,
    )(scal, q2, table, near, stats)


def solution(mesh):
    finer = Mesh(mesh.devices.reshape(8, 4, 4, 2, 2), SEQ + DOC)
    return jax.shard_map(
        on_device,
        mesh=finer,
        in_specs=(
            P(SEQ, DOC),
            P(SEQ, DOC),
            P(None, SEQ, DOC),
            P(None, DOC),
            P(None, DOC),
            P(None, DOC),
            P(None, SEQ),
        ),
        out_specs=P(SEQ, DOC),
        check_vma=False,
    )
```

```python
import jax
import jax.numpy as jnp
from jax import lax
from jax.experimental import pallas as pl
from jax.experimental.pallas import tpu as pltpu
from jax.sharding import Mesh
from jax.sharding import PartitionSpec as P


DH = 64
R = 256
W = 128
HEADS = 4
LANES = 128
ROWS = 8
SEQ = ("z", "yl", "x")
DOC = ("yh", "c")
EPS = 1e-05
LOW = -1e30
SWAP = [(0, 1), (1, 0)]

f32 = jnp.float32
bf16 = jnp.bfloat16
VMEM = pl.BlockSpec(memory_space=pltpu.VMEM)
SMEM = pl.BlockSpec(memory_space=pltpu.SMEM)


def call(kernel, out_shape, n_in, vmem_mib, flops, nbytes, exps=0):
    single = not isinstance(out_shape, (list, tuple))
    return pl.pallas_call(
        kernel,
        out_shape=out_shape,
        in_specs=[SMEM] + [VMEM] * n_in,
        out_specs=VMEM if single else [VMEM] * len(out_shape),
        compiler_params=pltpu.CompilerParams(vmem_limit_bytes=vmem_mib << 20),
        cost_estimate=pl.CostEstimate(flops=flops, bytes_accessed=nbytes, transcendentals=exps),
    )


def dot_nt(a, b):
    return lax.dot_general(a, b, (((1,), (1,)), ((), ())), preferred_element_type=f32)


def lanes_of(shape):
    return lax.broadcasted_iota(jnp.int32, shape, len(shape) - 1)


def prep_kernel(scal, q_ref, kv_ref, q2_ref, kvh_ref):
    tokens = q_ref.shape[0]
    local = scal[0]
    second = lax.broadcasted_iota(jnp.int32, (tokens, LANES), 0) >= local
    left = lanes_of((tokens, LANES)) < DH
    for pair in range(HEADS // 2):
        cols = slice(pair * LANES, (pair + 1) * LANES)
        query = q_ref[:, cols].astype(f32) * 0.125
        keys = kv_ref[0, :, cols].astype(f32)
        values = kv_ref[1, :, cols].astype(f32)
        query_r = pltpu.roll(query, DH, 1)
        keys_r = pltpu.roll(keys, DH, 1)
        values_r = pltpu.roll(values, DH, 1)
        for half in range(2):
            h = 2 * pair + half
            both = jnp.where(left, query, query_r) if half == 0 else jnp.where(left, query_r, query)
            q2_ref[h] = jnp.where(left == second, 0.0, both).astype(bf16)
            joined = jnp.where(left, keys, values_r) if half == 0 else jnp.where(left, keys_r, values)
            kvh_ref[h, :, :LANES] = jnp.where(second, 0.0, joined).astype(bf16)
            kvh_ref[h, :, LANES:] = jnp.where(second, joined, 0.0).astype(bf16)


def near_kernel(scal, q_ref, kv_ref, before_ref, after_ref, o_ref, top_ref, sum_ref):
    tokens = q_ref.shape[0]
    local, base, total = scal[0], scal[1], scal[2]
    blocks = tokens // W
    span = 3 * W
    row = lax.broadcasted_iota(jnp.int32, (W, span), 0)
    col = lax.broadcasted_iota(jnp.int32, (W, span), 1)
    band = (col >= row) & (col - row <= 2 * W)
    left = lanes_of((W, LANES)) < DH

    def piece(s, at, cols):
        if at < 0:
            return before_ref[s, :, cols]
        if at >= blocks:
            return after_ref[s, :, cols]
        return kv_ref[s, at * W : (at + 1) * W, cols]

    for b in range(blocks):
        query_pos = row + b * W
        key_pos = col + (b - 1) * W
        allowed = (
            band
            & ((query_pos >= local) == (key_pos >= local))
            & (key_pos + base >= 0)
            & (key_pos + base < total)
        )
        for pair in range(HEADS // 2):
            cols = slice(pair * LANES, (pair + 1) * LANES)
            query = q_ref[b * W : (b + 1) * W, cols].astype(f32) * 0.125
            keys = jnp.concatenate([piece(0, b + i, cols) for i in (-1, 0, 1)], axis=0)
            values = jnp.concatenate([piece(1, b + i, cols) for i in (-1, 0, 1)], axis=0)
            outs = []
            for half in range(2):
                h = 2 * pair + half
                mine = jnp.where(left == (half == 0), query, 0.0).astype(bf16)
                scores = jnp.where(allowed, dot_nt(mine, keys), LOW)
                top = jnp.max(scores, axis=1, keepdims=True)
                weight = jnp.exp(scores - top)
                total_w = jnp.sum(weight, axis=1, keepdims=True)
                outs.append(jnp.dot(weight.astype(bf16), values, preferred_element_type=f32))
                top_ref[h, b * W : (b + 1) * W] = jnp.broadcast_to(top, (W, LANES))
                sum_ref[h, b * W : (b + 1) * W] = jnp.broadcast_to(total_w, (W, LANES))
            o_ref[b * W : (b + 1) * W, cols] = jnp.where(left, outs[0], outs[1])


def pieces_of(top):
    a = top.astype(bf16).astype(f32)
    b = (top - a).astype(bf16).astype(f32)
    return a, b, top - a - b


def partial_kernel(scal, x0, x1, wt_ref, acc_ref):
    acc_ref[...] = dot_nt(wt_ref[scal[3]], x0[...]) + dot_nt(wt_ref[scal[4]], x1[...])


def more_kernel(scal, x2, wt_ref, acc_ref, out_ref):
    out_ref[...] = acc_ref[...] + dot_nt(wt_ref[scal[5]], x2[...])


def project_kernel(scal, x3, wt_ref, acc_ref, kvh_ref, out_ref, held, sems):
    tokens = x3.shape[0]
    local = scal[0]
    second = lax.broadcasted_iota(jnp.int32, (R, tokens), 1) >= local
    mixed = jnp.logical_and(local > 0, local < tokens)
    lane = lanes_of((R, LANES))
    at_a = lane == 0
    at_b = lane == DH
    left = lane < DH
    copies = []
    for h in range(HEADS):
        rows = slice(h * R, (h + 1) * R)
        logits = acc_ref[rows, :] + dot_nt(wt_ref[scal[6], rows, :], x3[...])
        top0 = jnp.maximum(jnp.max(jnp.where(second, LOW, logits), axis=1, keepdims=True), LOW)
        top1 = jnp.maximum(jnp.max(jnp.where(second, logits, LOW), axis=1, keepdims=True), LOW)
        a0, b0, c0 = pieces_of(top0)
        a1, b1, c1 = pieces_of(top1)
        proj = jnp.exp(logits - jnp.where(second, a1 + b1, a0 + b0)).astype(bf16)
        sums = jnp.dot(proj, kvh_ref[h], preferred_element_type=f32)
        n0 = sums[:, :LANES]
        n1 = sums[:, LANES:]
        n0 = n0 - jnp.where(left, n0[:, 0:1], n0[:, DH : DH + 1])
        n1 = n1 - jnp.where(left, n1[:, 0:1], n1[:, DH : DH + 1])
        late = local <= 0
        a_p, b_p, c_p = (jnp.where(late, u1, u0) for u0, u1 in ((a0, a1), (b0, b1), (c0, c1)))
        body = jnp.where(mixed, n0, n0 + n1)
        hi = body.astype(bf16).astype(f32)
        rest = jnp.where(mixed, n1, body - hi)
        hi = jnp.where(at_a, a_p, jnp.where(at_b, b_p, hi))
        rest = jnp.where(
            at_a,
            jnp.where(mixed, a1, c_p),
            jnp.where(at_b, jnp.where(mixed, b1, jnp.zeros_like(b1)), rest),
        )
        parts = R // ROWS
        packed = jnp.concatenate(
            [hi.reshape(parts, ROWS, LANES), rest.reshape(parts, ROWS, LANES)], axis=1
        )
        held[h] = packed.astype(bf16)
        copy = pltpu.make_async_copy(
            held.at[h], out_ref.at[pl.ds(h * parts, parts)], sems.at[h]
        )
        copy.start()
        copies.append(copy)
    for copy in copies:
        copy.wait()


def combine_kernel(scal, in_ref, gain_ref, bias_ref, out_ref):
    senders = in_ref.shape[0]
    split, tokens = scal[0], scal[1]
    edge = split // tokens
    has_edge = lax.rem(split, tokens) != 0
    shape = (senders, ROWS, LANES)
    j = lax.broadcasted_iota(jnp.int32, shape, 0)
    is_edge = jnp.logical_and(j == edge, has_edge)
    late = j * tokens >= split
    first = in_ref[:, :ROWS, :].astype(f32)
    other = in_ref[:, ROWS:, :].astype(f32)
    top = first[:, :, 0:1] + first[:, :, DH : DH + 1]
    top = jnp.broadcast_to(top, shape)
    fine = jnp.where(is_edge, 0.0, jnp.broadcast_to(other[:, :, 0:1], shape))
    value = jnp.where(is_edge, first, first + other)
    extra = in_ref[edge % senders].astype(f32)[ROWS:]
    extra_top = jnp.broadcast_to(extra[:, 0:1] + extra[:, DH : DH + 1], (ROWS, LANES))
    extra_top = jnp.where(has_edge, extra_top, LOW)
    top0 = jnp.max(jnp.where(late, LOW, top), axis=0)
    full0 = jnp.max(jnp.where(late, LOW, top + fine), axis=0)
    top1 = jnp.maximum(jnp.max(jnp.where(late, top, LOW), axis=0), extra_top)
    full1 = jnp.maximum(jnp.max(jnp.where(late, top + fine, LOW), axis=0), extra_top)
    weight = jnp.exp(top - jnp.where(late, top1[None], top0[None]))
    value = value * weight
    n0 = jnp.sum(jnp.where(late, 0.0, value), axis=0)
    n1 = jnp.sum(jnp.where(late, value, 0.0), axis=0)
    n1 = n1 + jnp.where(has_edge, extra * jnp.exp(extra_top - top1), 0.0)
    lane = lanes_of((ROWS, LANES))
    left = lane < DH
    used = jnp.logical_and(lane != 0, lane != DH)
    gain = gain_ref[...]
    bias = bias_ref[...]

    def halves(v):
        a = jnp.sum(jnp.where(left, v, 0.0), axis=1, keepdims=True)
        b = jnp.sum(jnp.where(left, 0.0, v), axis=1, keepdims=True)
        return jnp.where(left, a, b) * (1.0 / DH)

    def norm(n, top_v, full_v):
        n = jnp.where(used, n, 0.0)
        centred = n - halves(n)
        variance = halves(centred * centred)
        scale = jnp.exp(2.0 * (full_v - top_v))
        return centred * lax.rsqrt(variance + EPS * scale) * gain + bias

    t0 = norm(n0, top0, full0)
    t1 = norm(n1, top1, full1)
    keys = jnp.where(left, t0, pltpu.roll(t1, DH, 1))
    values = jnp.where(left, pltpu.roll(t0, DH, 1), t1)
    chunk = jnp.concatenate([keys, values], axis=0)[None]
    out_ref[...] = jnp.broadcast_to(chunk, out_ref.shape).astype(bf16)


def far_kernel(scal, q2_ref, tab_ref, o_ref, top_ref, sum_ref, out_ref):
    tokens = o_ref.shape[0]
    local = scal[0]
    shape = (tokens, LANES)
    left = lanes_of(shape) < DH
    second = lax.broadcasted_iota(jnp.int32, shape, 0) >= local
    parts = R // ROWS
    for pair in range(HEADS // 2):
        cols = slice(pair * LANES, (pair + 1) * LANES)
        near = o_ref[:, cols]
        outs = []
        for half in range(2):
            h = 2 * pair + half
            table = tab_ref[h * parts : (h + 1) * parts].astype(f32)
            keys = table[:, :ROWS].reshape(R, LANES).astype(bf16)
            values = table[:, ROWS:].reshape(R, LANES).astype(bf16)
            scores = dot_nt(q2_ref[h], keys)
            low, high = scores[:, :LANES], scores[:, LANES:]
            near_top = top_ref[h]
            top = jnp.max(jnp.maximum(low, high), axis=1, keepdims=True)
            top = jnp.maximum(jnp.broadcast_to(top, shape), near_top)
            low = jnp.exp(low - top)
            high = jnp.exp(high - top)
            scale = jnp.exp(near_top - top)
            total = jnp.broadcast_to(jnp.sum(low + high, axis=1, keepdims=True), shape)
            total = total + sum_ref[h] * scale
            weight = jnp.concatenate([low.astype(bf16), high.astype(bf16)], axis=1)
            far = jnp.dot(weight, values, preferred_element_type=f32)
            swap = second if half == 0 else jnp.logical_not(second)
            far = jnp.where(swap, pltpu.roll(far, DH, 1), far)
            outs.append((near * scale + far) / total)
        out_ref[:, cols] = jnp.where(left, outs[0], outs[1]).astype(bf16)


def on_device(inputs, queries, keys_values, slot_weight, slot_gain, slot_bias, bounds):
    tokens, width = inputs.shape
    shards = lax.axis_size(SEQ)
    shard = lax.axis_index(SEQ)
    split = jnp.where(bounds[0, 0] > 0, bounds[0, 0], bounds[1, 0])
    base = shard * tokens
    yh, c = lax.axis_index("yh"), lax.axis_index("c")
    scal = jnp.stack(
        [
            split - base,
            base,
            jnp.int32(shards * tokens),
            yh * 2 + c,
            yh * 2 + 1 - c,
            (1 - yh) * 2 + c,
            (1 - yh) * 2 + 1 - c,
        ]
    ).astype(jnp.int32)
    scal2 = jnp.stack([split, jnp.int32(tokens)]).astype(jnp.int32)

    x2 = lax.ppermute(inputs, "yh", SWAP)
    x1 = lax.ppermute(inputs, "c", SWAP)
    x3 = lax.ppermute(x2, "c", SWAP)
    up = [(i, i + 1) for i in range(shards - 1)]
    down = [(j, i) for i, j in up]
    before = lax.ppermute(keys_values[:, tokens - W :], SEQ, up)
    after = lax.ppermute(keys_values[:, :W], SEQ, down)

    weight_t = jnp.swapaxes(slot_weight.reshape(4, width, HEADS * R), 1, 2)
    q2, kvh = call(
        prep_kernel,
        [
            jax.ShapeDtypeStruct((HEADS, tokens, LANES), bf16),
            jax.ShapeDtypeStruct((HEADS, tokens, 2 * LANES), bf16),
        ],
        2, 16, 0, 3 << 20,
    )(scal, queries, keys_values)

    slots = HEADS * R
    flops = 2 * tokens * slots * width
    acc_shape = jax.ShapeDtypeStruct((slots, tokens), f32)
    acc = call(partial_kernel, acc_shape, 3, 16, 2 * flops, 5 << 20)(
        scal, inputs, x1, weight_t
    )
    acc = call(more_kernel, acc_shape, 3, 16, flops, 6 << 20)(scal, x2, weight_t, acc)
    sent = pl.pallas_call(
        project_kernel,
        out_shape=jax.ShapeDtypeStruct((shards, 2 * ROWS, LANES), bf16),
        in_specs=[SMEM] + [VMEM] * 4,
        out_specs=pl.BlockSpec(memory_space=pltpu.HBM),
        scratch_shapes=[
            pltpu.VMEM((HEADS, R // ROWS, 2 * ROWS, LANES), bf16),
            pltpu.SemaphoreType.DMA((HEADS,)),
        ],
        compiler_params=pltpu.CompilerParams(vmem_limit_bytes=24 << 20),
        cost_estimate=pl.CostEstimate(
            flops=2 * flops, bytes_accessed=5 << 20, transcendentals=tokens * slots
        ),
    )(scal, x3, weight_t, acc, kvh)
    arrived = lax.all_to_all(sent, SEQ, 0, 0, tiled=True)

    rep = jax.ShapeDtypeStruct((HEADS, tokens, LANES), f32)
    near, tops, sums = call(
        near_kernel,
        [jax.ShapeDtypeStruct((tokens, HEADS * DH), f32), rep, rep],
        4, 8, 4 * tokens * 3 * W * HEADS * LANES, 2 << 20, tokens * 3 * W * HEADS,
    )(scal, queries, keys_values, before, after)

    head = shard * ROWS // R
    gain = lax.dynamic_slice_in_dim(slot_gain, head * DH, DH, 1).reshape(1, 2 * DH)
    bias = lax.dynamic_slice_in_dim(slot_bias, head * DH, DH, 1).reshape(1, 2 * DH)
    chunk = call(
        combine_kernel,
        jax.ShapeDtypeStruct((shards, 2 * ROWS, LANES), bf16),
        3, 8, 0, 1 << 20, 1 << 17,
    )(scal2, arrived, gain, bias)
    table = lax.all_to_all(chunk, SEQ, 0, 0, tiled=True)

    return call(
        far_kernel,
        jax.ShapeDtypeStruct((tokens, HEADS * DH), bf16),
        5, 12, 4 * tokens * R * HEADS * LANES, 2 << 20, tokens * R * HEADS,
    )(scal, q2, table, near, tops, sums)


def solution(mesh):
    finer = Mesh(mesh.devices.reshape(8, 4, 4, 2, 2), SEQ + DOC)
    return jax.shard_map(
        on_device,
        mesh=finer,
        in_specs=(
            P(SEQ, DOC),
            P(SEQ, DOC),
            P(None, SEQ, DOC),
            P(None, DOC),
            P(None, DOC),
            P(None, DOC),
            P(None, SEQ),
        ),
        out_specs=P(SEQ, DOC),
        check_vma=False,
    )
```

```python
import jax
import jax.numpy as jnp
from jax import lax
from jax.experimental import pallas as pl
from jax.experimental.pallas import tpu as pltpu
from jax.sharding import Mesh
from jax.sharding import PartitionSpec as P


DH = 64
R = 256
W = 128
HEADS = 4
LANES = 128
ROWS = 32
RING = ("z", "x")
LINE = "yl"
SEQ = ("z", "yl", "x")
DOC = ("yh", "c")
EPS = 1e-05
LOW = -1e30
SWAP = [(0, 1), (1, 0)]

f32 = jnp.float32
bf16 = jnp.bfloat16
VMEM = pl.BlockSpec(memory_space=pltpu.VMEM)
SMEM = pl.BlockSpec(memory_space=pltpu.SMEM)


def call(kernel, out_shape, n_in, vmem_mib, flops, nbytes, exps=0):
    single = not isinstance(out_shape, (list, tuple))
    return pl.pallas_call(
        kernel,
        out_shape=out_shape,
        in_specs=[SMEM] + [VMEM] * n_in,
        out_specs=VMEM if single else [VMEM] * len(out_shape),
        compiler_params=pltpu.CompilerParams(vmem_limit_bytes=vmem_mib << 20),
        cost_estimate=pl.CostEstimate(flops=flops, bytes_accessed=nbytes, transcendentals=exps),
    )


def dot_nt(a, b):
    return lax.dot_general(a, b, (((1,), (1,)), ((), ())), preferred_element_type=f32)


def lanes_of(shape):
    return lax.broadcasted_iota(jnp.int32, shape, len(shape) - 1)


def prep_kernel(scal, kv_ref, kvh_ref):
    tokens = kv_ref.shape[1]
    local = scal[0]
    second = lax.broadcasted_iota(jnp.int32, (tokens, LANES), 0) >= local
    left = lanes_of((tokens, LANES)) < DH
    for pair in range(HEADS // 2):
        cols = slice(pair * LANES, (pair + 1) * LANES)
        keys = kv_ref[0, :, cols].astype(f32)
        values = kv_ref[1, :, cols].astype(f32)
        keys_r = pltpu.roll(keys, DH, 1)
        values_r = pltpu.roll(values, DH, 1)
        for half in range(2):
            h = 2 * pair + half
            joined = jnp.where(left, keys, values_r) if half == 0 else jnp.where(left, keys_r, values)
            kvh_ref[h, :, :LANES] = jnp.where(second, 0.0, joined).astype(bf16)
            kvh_ref[h, :, LANES:] = jnp.where(second, joined, 0.0).astype(bf16)


def near_kernel(scal, q_ref, kv_ref, before_ref, after_ref, o_ref, stat_ref, q2_ref):
    tokens = q_ref.shape[0]
    local, base, total = scal[0], scal[1], scal[2]
    blocks = tokens // W
    span = 3 * W
    row = lax.broadcasted_iota(jnp.int32, (W, span), 0)
    col = lax.broadcasted_iota(jnp.int32, (W, span), 1)
    band = (col >= row) & (col - row <= 2 * W)
    left = lanes_of((W, LANES)) < DH
    place = lax.broadcasted_iota(jnp.int32, (W, LANES), 0)

    def piece(s, at, cols):
        if at < 0:
            return before_ref[s, :, cols]
        if at >= blocks:
            return after_ref[s, :, cols]
        return kv_ref[s, at * W : (at + 1) * W, cols]

    for b in range(blocks):
        query_pos = row + b * W
        key_pos = col + (b - 1) * W
        allowed = (
            band
            & ((query_pos >= local) == (key_pos >= local))
            & (key_pos + base >= 0)
            & (key_pos + base < total)
        )
        for pair in range(HEADS // 2):
            cols = slice(pair * LANES, (pair + 1) * LANES)
            query = q_ref[b * W : (b + 1) * W, cols].astype(f32) * 0.125
            query_r = pltpu.roll(query, DH, 1)
            second = place + b * W >= local
            keys = jnp.concatenate([piece(0, b + i, cols) for i in (-1, 0, 1)], axis=0)
            values = jnp.concatenate([piece(1, b + i, cols) for i in (-1, 0, 1)], axis=0)
            outs = []
            for half in range(2):
                h = 2 * pair + half
                both = jnp.where(left, query, query_r) if half == 0 else jnp.where(left, query_r, query)
                q2_ref[h, b * W : (b + 1) * W] = jnp.where(left == second, 0.0, both).astype(bf16)
                mine = jnp.where(left if half == 0 else jnp.logical_not(left), query, 0.0).astype(bf16)
                scores = jnp.where(allowed, dot_nt(mine, keys), LOW)
                top = jnp.max(scores, axis=1, keepdims=True)
                weight = jnp.exp(scores - top)
                total_w = jnp.sum(weight, axis=1, keepdims=True)
                outs.append(jnp.dot(weight.astype(bf16), values, preferred_element_type=f32))
                stat_ref[h, b * W : (b + 1) * W] = jnp.where(left, top, total_w)
            o_ref[b * W : (b + 1) * W, cols] = jnp.where(left, outs[0], outs[1])


def pieces_of(top):
    a = top.astype(bf16).astype(f32)
    b = (top - a).astype(bf16).astype(f32)
    return a, b, top - a - b


def partial_kernel(scal, x0, x1, wt_ref, acc_ref):
    acc_ref[...] = dot_nt(wt_ref[scal[3]], x0[...]) + dot_nt(wt_ref[scal[4]], x1[...])


def more_kernel(scal, x2, wt_ref, acc_ref, out_ref):
    out_ref[...] = acc_ref[...] + dot_nt(wt_ref[scal[5]], x2[...])


def project_kernel(scal, x3, wt_ref, acc_ref, kvh_ref, out_ref, held, sems):
    tokens = x3.shape[0]
    local = scal[0]
    second = lax.broadcasted_iota(jnp.int32, (R, tokens), 1) >= local
    mixed = jnp.logical_and(local > 0, local < tokens)
    lane = lanes_of((R, LANES))
    at_a = lane == 0
    at_b = lane == DH
    left = lane < DH
    copies = []
    for h in range(HEADS):
        rows = slice(h * R, (h + 1) * R)
        logits = acc_ref[rows, :] + dot_nt(wt_ref[scal[6], rows, :], x3[...])
        top0 = jnp.maximum(jnp.max(jnp.where(second, LOW, logits), axis=1, keepdims=True), LOW)
        top1 = jnp.maximum(jnp.max(jnp.where(second, logits, LOW), axis=1, keepdims=True), LOW)
        a0, b0, c0 = pieces_of(top0)
        a1, b1, c1 = pieces_of(top1)
        proj = jnp.exp(logits - jnp.where(second, a1 + b1, a0 + b0)).astype(bf16)
        sums = jnp.dot(proj, kvh_ref[h], preferred_element_type=f32)
        n0 = sums[:, :LANES]
        n1 = sums[:, LANES:]
        n0 = n0 - jnp.where(left, n0[:, 0:1], n0[:, DH : DH + 1])
        n1 = n1 - jnp.where(left, n1[:, 0:1], n1[:, DH : DH + 1])
        late = local <= 0
        a_p, b_p, c_p = (jnp.where(late, u1, u0) for u0, u1 in ((a0, a1), (b0, b1), (c0, c1)))
        body = jnp.where(mixed, n0, n0 + n1)
        hi = body.astype(bf16).astype(f32)
        rest = jnp.where(mixed, n1, body - hi)
        hi = jnp.where(at_a, a_p, jnp.where(at_b, b_p, hi))
        rest = jnp.where(
            at_a,
            jnp.where(mixed, a1, c_p),
            jnp.where(at_b, jnp.where(mixed, b1, jnp.zeros_like(b1)), rest),
        )
        parts = R // ROWS
        packed = jnp.concatenate(
            [hi.reshape(parts, ROWS, LANES), rest.reshape(parts, ROWS, LANES)], axis=1
        )
        held[h] = packed.astype(bf16)
        copy = pltpu.make_async_copy(
            held.at[h], out_ref.at[pl.ds(h * parts, parts)], sems.at[h]
        )
        copy.start()
        copies.append(copy)
    for copy in copies:
        copy.wait()


def combine_kernel(scal, in_ref, out_ref):
    senders = in_ref.shape[0]
    split, tokens, line, lines, ring = scal[0], scal[1], scal[2], scal[3], scal[4]
    edge = lax.div(split, tokens)
    has_edge = jnp.logical_and(
        lax.rem(split, tokens) != 0, lax.rem(lax.div(edge, ring), lines) == line
    )
    slot = lax.div(edge, ring * lines) * ring + lax.rem(edge, ring)
    slot = jnp.where(has_edge, slot, 0)
    shape = (senders, ROWS, LANES)
    k = lax.broadcasted_iota(jnp.int32, shape, 0)
    is_edge = jnp.logical_and(k == slot, has_edge)
    j = lax.div(k, ring) * (ring * lines) + line * ring + lax.rem(k, ring)
    late = j * tokens >= split
    first = in_ref[:, :ROWS, :].astype(f32)
    other = in_ref[:, ROWS:, :].astype(f32)
    top = jnp.broadcast_to(first[:, :, 0:1] + first[:, :, DH : DH + 1], shape)
    fine = jnp.where(is_edge, 0.0, jnp.broadcast_to(other[:, :, 0:1], shape))
    value = jnp.where(is_edge, first, first + other)
    extra = in_ref[slot].astype(f32)[ROWS:]
    extra_top = jnp.broadcast_to(extra[:, 0:1] + extra[:, DH : DH + 1], (ROWS, LANES))
    extra_top = jnp.where(has_edge, extra_top, LOW)
    top0 = jnp.max(jnp.where(late, LOW, top), axis=0)
    full0 = jnp.max(jnp.where(late, LOW, top + fine), axis=0)
    top1 = jnp.maximum(jnp.max(jnp.where(late, top, LOW), axis=0), extra_top)
    full1 = jnp.maximum(jnp.max(jnp.where(late, top + fine, LOW), axis=0), extra_top)
    weight = jnp.exp(top - jnp.where(late, top1[None], top0[None]))
    value = value * weight
    n0 = jnp.sum(jnp.where(late, 0.0, value), axis=0)
    n1 = jnp.sum(jnp.where(late, value, 0.0), axis=0)
    n1 = n1 + jnp.where(has_edge, extra * jnp.exp(extra_top - top1), 0.0)
    lane = lanes_of((ROWS, LANES))
    n0 = jnp.where(lane == 0, top0, jnp.where(lane == DH, full0, n0))
    n1 = jnp.where(lane == 0, top1, jnp.where(lane == DH, full1, n1))
    out_ref[...] = jnp.broadcast_to(jnp.concatenate([n0, n1], axis=0)[None], out_ref.shape)


def norm_kernel(scal, in_ref, gain_ref, bias_ref, out_ref):
    got = in_ref[...]
    top = jnp.broadcast_to(got[:, :, 0:1], got.shape)
    whole = jnp.max(top, axis=0)
    full = jnp.max(jnp.broadcast_to(got[:, :, DH : DH + 1], got.shape), axis=0)
    n = jnp.sum(got * jnp.exp(top - whole[None]), axis=0)
    lane = lanes_of((2 * ROWS, LANES))
    left = lane < DH
    used = jnp.logical_and(lane != 0, lane != DH)

    def halves(v):
        a = jnp.sum(jnp.where(left, v, 0.0), axis=1, keepdims=True)
        b = jnp.sum(jnp.where(left, 0.0, v), axis=1, keepdims=True)
        return jnp.where(left, a, b) * (1.0 / DH)

    n = jnp.where(used, n, 0.0)
    centred = n - halves(n)
    variance = halves(centred * centred)
    scale = jnp.exp(2.0 * (full - whole))
    table = centred * lax.rsqrt(variance + EPS * scale) * gain_ref[...] + bias_ref[...]
    t0, t1 = table[:ROWS], table[ROWS:]
    left = left[:ROWS]
    keys = jnp.where(left, t0, pltpu.roll(t1, DH, 1))
    values = jnp.where(left, pltpu.roll(t0, DH, 1), t1)
    chunk = jnp.concatenate([keys, values], axis=0).astype(bf16)[None]
    out_ref[...] = jnp.broadcast_to(chunk, out_ref.shape)


def far_kernel(scal, q2_ref, tab_ref, o_ref, stat_ref, out_ref):
    tokens = o_ref.shape[0]
    local = scal[0]
    shape = (tokens, LANES)
    left = lanes_of(shape) < DH
    second = lax.broadcasted_iota(jnp.int32, shape, 0) >= local
    parts = R // ROWS
    for pair in range(HEADS // 2):
        cols = slice(pair * LANES, (pair + 1) * LANES)
        near = o_ref[:, cols]
        outs = []
        for half in range(2):
            h = 2 * pair + half
            keys = tab_ref[h * parts : (h + 1) * parts, :ROWS].reshape(R, LANES)
            values = tab_ref[h * parts : (h + 1) * parts, ROWS:].reshape(R, LANES)
            scores = dot_nt(q2_ref[h], keys)
            low, high = scores[:, :LANES], scores[:, LANES:]
            stat = stat_ref[h]
            stat_r = pltpu.roll(stat, DH, 1)
            near_top = jnp.where(left, stat, stat_r)
            top = jnp.max(jnp.maximum(low, high), axis=1, keepdims=True)
            top = jnp.maximum(jnp.broadcast_to(top, shape), near_top)
            low = jnp.exp(low - top)
            high = jnp.exp(high - top)
            scale = jnp.exp(near_top - top)
            total = jnp.broadcast_to(jnp.sum(low + high, axis=1, keepdims=True), shape)
            total = total + jnp.where(left, stat_r, stat) * scale
            weight = jnp.concatenate([low.astype(bf16), high.astype(bf16)], axis=1)
            far = jnp.dot(weight, values, preferred_element_type=f32)
            swap = second if half == 0 else jnp.logical_not(second)
            far = jnp.where(swap, pltpu.roll(far, DH, 1), far)
            outs.append((near * scale + far) / total)
        out_ref[:, cols] = jnp.where(left, outs[0], outs[1]).astype(bf16)


def on_device(inputs, queries, keys_values, slot_weight, slot_gain, slot_bias, bounds):
    tokens, width = inputs.shape
    shards = lax.axis_size(SEQ)
    shard = lax.axis_index(SEQ)
    split = jnp.where(bounds[0, 0] > 0, bounds[0, 0], bounds[1, 0])
    base = shard * tokens
    yh, c = lax.axis_index("yh"), lax.axis_index("c")
    scal = jnp.stack(
        [
            split - base,
            base,
            jnp.int32(shards * tokens),
            yh * 2 + c,
            yh * 2 + 1 - c,
            (1 - yh) * 2 + c,
            (1 - yh) * 2 + 1 - c,
        ]
    ).astype(jnp.int32)
    line = lax.axis_index(LINE)
    slot = lax.axis_index(RING)
    lines = lax.axis_size(LINE)
    slots_held = lax.axis_size(RING)
    scal2 = jnp.stack(
        [split, jnp.int32(tokens), line, jnp.int32(lines), jnp.int32(lax.axis_size("x"))]
    ).astype(jnp.int32)

    x2 = lax.ppermute(inputs, "yh", SWAP)
    x1 = lax.ppermute(inputs, "c", SWAP)
    x3 = lax.ppermute(x2, "c", SWAP)
    up = [(i, i + 1) for i in range(shards - 1)]
    down = [(j, i) for i, j in up]
    before = lax.ppermute(keys_values[:, tokens - W :], SEQ, up)
    after = lax.ppermute(keys_values[:, :W], SEQ, down)

    weight_t = jnp.swapaxes(slot_weight.reshape(4, width, HEADS * R), 1, 2)
    kvh = call(
        prep_kernel,
        jax.ShapeDtypeStruct((HEADS, tokens, 2 * LANES), bf16),
        1, 8, 0, 2 << 20,
    )(scal, keys_values)

    slots = HEADS * R
    flops = 2 * tokens * slots * width
    acc_shape = jax.ShapeDtypeStruct((slots, tokens), f32)
    acc = call(partial_kernel, acc_shape, 3, 16, 2 * flops, 5 << 20)(
        scal, inputs, x1, weight_t
    )
    acc = call(more_kernel, acc_shape, 3, 16, flops, 6 << 20)(scal, x2, weight_t, acc)
    sent = pl.pallas_call(
        project_kernel,
        out_shape=jax.ShapeDtypeStruct((slots_held, 2 * ROWS, LANES), bf16),
        in_specs=[SMEM] + [VMEM] * 4,
        out_specs=pl.BlockSpec(memory_space=pltpu.HBM),
        scratch_shapes=[
            pltpu.VMEM((HEADS, R // ROWS, 2 * ROWS, LANES), bf16),
            pltpu.SemaphoreType.DMA((HEADS,)),
        ],
        compiler_params=pltpu.CompilerParams(vmem_limit_bytes=24 << 20),
        cost_estimate=pl.CostEstimate(
            flops=2 * flops, bytes_accessed=5 << 20, transcendentals=tokens * slots
        ),
    )(scal, x3, weight_t, acc, kvh)
    arrived = lax.all_to_all(sent, RING, 0, 0, tiled=True)

    near, stats, q2 = call(
        near_kernel,
        [
            jax.ShapeDtypeStruct((tokens, HEADS * DH), f32),
            jax.ShapeDtypeStruct((HEADS, tokens, LANES), f32),
            jax.ShapeDtypeStruct((HEADS, tokens, LANES), bf16),
        ],
        4, 8, 4 * tokens * 3 * W * HEADS * LANES, 2 << 20, tokens * 3 * W * HEADS,
    )(scal, queries, keys_values, before, after)

    held = call(
        combine_kernel,
        jax.ShapeDtypeStruct((lines, 2 * ROWS, LANES), f32),
        1, 8, 0, 1 << 20, 1 << 17,
    )(scal2, arrived)
    shared = lax.all_to_all(held, LINE, 0, 0, tiled=True)
    head = lax.div(slot * ROWS, R)
    gain = lax.dynamic_slice_in_dim(slot_gain, head * DH, DH, 1).reshape(1, 2 * DH)
    bias = lax.dynamic_slice_in_dim(slot_bias, head * DH, DH, 1).reshape(1, 2 * DH)
    chunk = call(
        norm_kernel,
        jax.ShapeDtypeStruct((slots_held, 2 * ROWS, LANES), bf16),
        3, 8, 0, 1 << 20, 1 << 15,
    )(scal2, shared, gain, bias)
    table = lax.all_to_all(chunk, RING, 0, 0, tiled=True)

    return call(
        far_kernel,
        jax.ShapeDtypeStruct((tokens, HEADS * DH), bf16),
        4, 12, 4 * tokens * R * HEADS * LANES, 2 << 20, tokens * R * HEADS,
    )(scal, q2, table, near, stats)


def solution(mesh):
    finer = Mesh(mesh.devices.reshape(8, 4, 4, 2, 2), SEQ + DOC)
    return jax.shard_map(
        on_device,
        mesh=finer,
        in_specs=(
            P(SEQ, DOC),
            P(SEQ, DOC),
            P(None, SEQ, DOC),
            P(None, DOC),
            P(None, DOC),
            P(None, DOC),
            P(None, SEQ),
        ),
        out_specs=P(SEQ, DOC),
        check_vma=False,
    )
```

```python
import functools

import jax
import jax.numpy as jnp
from jax import lax
from jax.experimental import pallas as pl
from jax.experimental.pallas import tpu as pltpu
from jax.sharding import Mesh
from jax.sharding import PartitionSpec as P


DH = 64
R = 256
W = 128
HEADS = 4
LANES = 128
ROWS = 32
RING = ("z", "x")
LINE = "yl"
SEQ = ("z", "yl", "x")
DOC = ("yh", "c")
EPS = 1e-05
LOW = -1e30
SWAP = [(0, 1), (1, 0)]

f32 = jnp.float32
bf16 = jnp.bfloat16
VMEM = pl.BlockSpec(memory_space=pltpu.VMEM)
SMEM = pl.BlockSpec(memory_space=pltpu.SMEM)


def call(kernel, out_shape, n_in, vmem_mib, flops, nbytes, exps=0, scalars=1, scratch=()):
    single = not isinstance(out_shape, (list, tuple))
    return pl.pallas_call(
        kernel,
        out_shape=out_shape,
        in_specs=[SMEM] * scalars + [VMEM] * n_in,
        out_specs=VMEM if single else [VMEM] * len(out_shape),
        scratch_shapes=list(scratch),
        compiler_params=pltpu.CompilerParams(vmem_limit_bytes=vmem_mib << 20),
        cost_estimate=pl.CostEstimate(flops=flops, bytes_accessed=nbytes, transcendentals=exps),
    )


def dot_nt(a, b):
    return lax.dot_general(a, b, (((1,), (1,)), ((), ())), preferred_element_type=f32)


def dot_tn(a, b):
    return lax.dot_general(a, b, (((0,), (0,)), ((), ())), preferred_element_type=f32)


def lanes_of(shape):
    return lax.broadcasted_iota(jnp.int32, shape, len(shape) - 1)


def prep_kernel(scal, kv_ref, kvh_ref):
    tokens = kv_ref.shape[1]
    local = scal[0]
    second = lax.broadcasted_iota(jnp.int32, (tokens, LANES), 0) >= local
    left = lanes_of((tokens, LANES)) < DH
    for pair in range(HEADS // 2):
        cols = slice(pair * LANES, (pair + 1) * LANES)
        keys = kv_ref[0, :, cols].astype(f32)
        values = kv_ref[1, :, cols].astype(f32)
        keys_r = pltpu.roll(keys, DH, 1)
        values_r = pltpu.roll(values, DH, 1)
        for half in range(2):
            h = 2 * pair + half
            joined = jnp.where(left, keys, values_r) if half == 0 else jnp.where(left, keys_r, values)
            kvh_ref[h, :, :LANES] = jnp.where(second, 0.0, joined).astype(bf16)
            kvh_ref[h, :, LANES:] = jnp.where(second, joined, 0.0).astype(bf16)


def near_kernel(scal, q_ref, kv_ref, before_ref, after_ref, o_ref, stat_ref, q2_ref):
    tokens = q_ref.shape[0]
    local, base, total = scal[0], scal[1], scal[2]
    blocks = tokens // W
    span = 3 * W
    key = lax.broadcasted_iota(jnp.int32, (span, W), 0)
    query_at = lax.broadcasted_iota(jnp.int32, (span, W), 1)
    band = (key >= query_at) & (key - query_at <= 2 * W)
    left = lanes_of((W, LANES)) < DH
    place = lax.broadcasted_iota(jnp.int32, (W, LANES), 0)
    stat_ref[...] = jnp.zeros_like(stat_ref)

    def piece(s, at, cols):
        if at < 0:
            return before_ref[s, :, cols]
        if at >= blocks:
            return after_ref[s, :, cols]
        return kv_ref[s, at * W : (at + 1) * W, cols]

    for b in range(blocks):
        here = slice(b * W, (b + 1) * W)
        query_pos = query_at + b * W
        key_pos = key + (b - 1) * W
        allowed = (
            band
            & ((query_pos >= local) == (key_pos >= local))
            & (key_pos + base >= 0)
            & (key_pos + base < total)
        )
        second = place + b * W >= local
        stat_ref[HEADS : HEADS + 1, here] = jnp.where(query_pos[:1] >= local, 1.0, 0.0)
        for pair in range(HEADS // 2):
            cols = slice(pair * LANES, (pair + 1) * LANES)
            query = q_ref[here, cols].astype(f32) * 0.125
            query_r = pltpu.roll(query, DH, 1)
            keys = jnp.concatenate([piece(0, b + i, cols) for i in (-1, 0, 1)], axis=0)
            values = jnp.concatenate([piece(1, b + i, cols) for i in (-1, 0, 1)], axis=0)
            for half in range(2):
                h = 2 * pair + half
                both = jnp.where(left, query, query_r) if half == 0 else jnp.where(left, query_r, query)
                q2_ref[h, here] = jnp.where(left == second, 0.0, both).astype(bf16)
                mine = jnp.where(left if half == 0 else jnp.logical_not(left), query, 0.0).astype(bf16)
                scores = jnp.where(allowed, dot_nt(keys, mine), LOW)
                top = jnp.max(scores, axis=0, keepdims=True)
                weight = jnp.exp(scores - top)
                stat_ref[h : h + 1, here] = top
                stat_ref[2 * HEADS + h : 2 * HEADS + h + 1, here] = jnp.sum(
                    weight, axis=0, keepdims=True
                )
                out = dot_tn(values, weight.astype(bf16))
                o_ref[h * DH : (h + 1) * DH, here] = out[half * DH : (half + 1) * DH]


def pieces_of(top):
    a = top.astype(bf16).astype(f32)
    b = (top - a).astype(bf16).astype(f32)
    return a, b, top - a - b


def partial_kernel(scal, x0, x1, wt_ref, acc_ref):
    acc_ref[...] = dot_nt(wt_ref[scal[3]], x0[...]) + dot_nt(wt_ref[scal[4]], x1[...])


def more_kernel(scal, x2, wt_ref, acc_ref, out_ref):
    out_ref[...] = acc_ref[...] + dot_nt(wt_ref[scal[5]], x2[...])


def project_kernel(scal, x3, wt_ref, acc_ref, kvh_ref, out_ref, held, sems):
    tokens = x3.shape[0]
    local = scal[0]
    mixed = jnp.logical_and(local > 0, local < tokens)
    lane = lanes_of((R, LANES))
    at_a = lane == 0
    at_b = lane == DH
    left = lane < DH
    parts = R // ROWS

    def logits_of(h):
        rows = slice(h * R, (h + 1) * R)
        return acc_ref[rows, :] + dot_nt(wt_ref[scal[6], rows, :], x3[...])

    def from_first(n):
        return n - jnp.where(left, n[:, 0:1], n[:, DH : DH + 1])

    def put(h, hi, rest):
        packed = jnp.concatenate(
            [hi.reshape(parts, ROWS, LANES), rest.reshape(parts, ROWS, LANES)], axis=1
        )
        held[h] = packed.astype(bf16)
        copy = pltpu.make_async_copy(
            held.at[h], out_ref.at[pl.ds(h * parts, parts)], sems.at[h]
        )
        copy.start()
        return copy

    @pl.when(jnp.logical_not(mixed))
    def _():
        side = pl.multiple_of(jnp.where(local <= 0, LANES, 0), LANES)
        copies = []
        for h in range(HEADS):
            logits = logits_of(h)
            a, b, c = pieces_of(jnp.max(logits, axis=1, keepdims=True))
            proj = jnp.exp(logits - (a + b)).astype(bf16)
            n = from_first(
                jnp.dot(proj, kvh_ref[h, :, pl.ds(side, LANES)], preferred_element_type=f32)
            )
            hi = n.astype(bf16).astype(f32)
            rest = jnp.where(at_a, c, jnp.where(at_b, 0.0, n - hi))
            hi = jnp.where(at_a, a, jnp.where(at_b, b, hi))
            copies.append(put(h, hi, rest))
        for copy in copies:
            copy.wait()

    @pl.when(mixed)
    def _():
        second = lax.broadcasted_iota(jnp.int32, (R, tokens), 1) >= local
        copies = []
        for h in range(HEADS):
            logits = logits_of(h)
            a0, b0, _ = pieces_of(jnp.max(jnp.where(second, LOW, logits), axis=1, keepdims=True))
            a1, b1, _ = pieces_of(jnp.max(jnp.where(second, logits, LOW), axis=1, keepdims=True))
            proj = jnp.exp(logits - jnp.where(second, a1 + b1, a0 + b0)).astype(bf16)
            sums = jnp.dot(proj, kvh_ref[h], preferred_element_type=f32)
            n0 = from_first(sums[:, :LANES])
            n1 = from_first(sums[:, LANES:])
            n0 = jnp.where(at_a, a0, jnp.where(at_b, b0, n0))
            n1 = jnp.where(at_a, a1, jnp.where(at_b, b1, n1))
            copies.append(put(h, n0, n1))
        for copy in copies:
            copy.wait()


def combine_kernel(lines, ring, tokens, scal, in_ref, out_ref, tops):
    senders = in_ref.shape[0]
    split, line = scal[0], scal[1]
    edge = lax.div(split, tokens)
    has_edge = jnp.logical_and(
        lax.rem(split, tokens) != 0, lax.rem(lax.div(edge, ring), lines) == line
    )
    slot = lax.div(edge, ring * lines) * ring + lax.rem(edge, ring)
    slot = jnp.where(has_edge, slot, 0)
    shape = (ROWS, LANES)
    low = jnp.full(shape, LOW, f32)
    extra = in_ref[slot, ROWS:].astype(f32)
    extra_top = jnp.broadcast_to(extra[:, 0:1] + extra[:, DH : DH + 1], shape)
    extra_top = jnp.where(has_edge, extra_top, low)
    top0, full0, top1, full1 = low, low, extra_top, extra_top
    late, is_edge = [], []
    for k in range(senders):
        j = (k // ring) * (ring * lines) + k % ring + line * ring
        late.append(j * tokens >= split)
        is_edge.append(jnp.logical_and(has_edge, slot == k))
        first = in_ref[k, :ROWS].astype(f32)
        other = in_ref[k, ROWS:].astype(f32)
        top = jnp.broadcast_to(first[:, 0:1] + first[:, DH : DH + 1], shape)
        full = top + jnp.where(is_edge[k], 0.0, jnp.broadcast_to(other[:, 0:1], shape))
        tops[k] = top
        top0 = jnp.maximum(top0, jnp.where(late[k], low, top))
        full0 = jnp.maximum(full0, jnp.where(late[k], low, full))
        top1 = jnp.maximum(top1, jnp.where(late[k], top, low))
        full1 = jnp.maximum(full1, jnp.where(late[k], full, low))
    n0 = jnp.zeros(shape, f32)
    n1 = jnp.where(has_edge, extra * jnp.exp(extra_top - top1), 0.0)
    for k in range(senders):
        first = in_ref[k, :ROWS].astype(f32)
        other = in_ref[k, ROWS:].astype(f32)
        value = first + jnp.where(is_edge[k], 0.0, other)
        value = value * jnp.exp(tops[k] - jnp.where(late[k], top1, top0))
        n0 = n0 + jnp.where(late[k], 0.0, value)
        n1 = n1 + jnp.where(late[k], value, 0.0)
    lane = lanes_of(shape)
    n0 = jnp.where(lane == 0, top0, jnp.where(lane == DH, full0, n0))
    n1 = jnp.where(lane == 0, top1, jnp.where(lane == DH, full1, n1))
    out_ref[...] = jnp.broadcast_to(jnp.concatenate([n0, n1], axis=0)[None], out_ref.shape)


def norm_kernel(in_ref, gain_ref, bias_ref, out_ref):
    got = in_ref[...]
    top = jnp.broadcast_to(got[:, :, 0:1], got.shape)
    whole = jnp.max(top, axis=0)
    full = jnp.max(jnp.broadcast_to(got[:, :, DH : DH + 1], got.shape), axis=0)
    n = jnp.sum(got * jnp.exp(top - whole[None]), axis=0)
    lane = lanes_of((2 * ROWS, LANES))
    left = lane < DH
    used = jnp.logical_and(lane != 0, lane != DH)

    def halves(v):
        a = jnp.sum(jnp.where(left, v, 0.0), axis=1, keepdims=True)
        b = jnp.sum(jnp.where(left, 0.0, v), axis=1, keepdims=True)
        return jnp.where(left, a, b) * (1.0 / DH)

    n = jnp.where(used, n, 0.0)
    centred = n - halves(n)
    variance = halves(centred * centred)
    scale = jnp.exp(2.0 * (full - whole))
    table = centred * lax.rsqrt(variance + EPS * scale) * gain_ref[...] + bias_ref[...]
    t0, t1 = table[:ROWS], table[ROWS:]
    left = left[:ROWS]
    keys = jnp.where(left, t0, pltpu.roll(t1, DH, 1))
    values = jnp.where(left, pltpu.roll(t0, DH, 1), t1)
    chunk = jnp.concatenate([keys, values], axis=0).astype(bf16)[None]
    out_ref[...] = jnp.broadcast_to(chunk, out_ref.shape)


def far_kernel(q2_ref, tab_ref, o_ref, stat_ref, out_ref):
    parts = R // ROWS
    second = stat_ref[HEADS : HEADS + 1, :] > 0.5
    for pair in range(HEADS // 2):
        outs = []
        for half in range(2):
            h = 2 * pair + half
            keys = tab_ref[h * parts : (h + 1) * parts, :ROWS].reshape(R, LANES)
            values = tab_ref[h * parts : (h + 1) * parts, ROWS:].reshape(R, LANES)
            scores = dot_nt(keys, q2_ref[h])
            near_top = stat_ref[h : h + 1, :]
            near_total = stat_ref[2 * HEADS + h : 2 * HEADS + h + 1, :]
            top = jnp.maximum(jnp.max(scores, axis=0, keepdims=True), near_top)
            weight = jnp.exp(scores - top)
            scale = jnp.exp(near_top - top)
            total = jnp.sum(weight, axis=0, keepdims=True) + near_total * scale
            far = dot_tn(values, weight.astype(bf16))
            far = jnp.where(second, far[DH:], far[:DH])
            outs.append((o_ref[h * DH : (h + 1) * DH] * scale + far) / total)
        both = jnp.concatenate(outs, axis=0)
        out_ref[:, pair * LANES : (pair + 1) * LANES] = jnp.transpose(both).astype(bf16)


def on_device(inputs, queries, keys_values, slot_weight, slot_gain, slot_bias, bounds):
    tokens, width = inputs.shape
    shards = lax.axis_size(SEQ)
    shard = lax.axis_index(SEQ)
    split = jnp.where(bounds[0, 0] > 0, bounds[0, 0], bounds[1, 0])
    base = shard * tokens
    yh, c = lax.axis_index("yh"), lax.axis_index("c")
    scal = jnp.stack(
        [
            split - base,
            base,
            jnp.int32(shards * tokens),
            yh * 2 + c,
            yh * 2 + 1 - c,
            (1 - yh) * 2 + c,
            (1 - yh) * 2 + 1 - c,
        ]
    ).astype(jnp.int32)
    line = lax.axis_index(LINE)
    slot = lax.axis_index(RING)
    lines = lax.axis_size(LINE)
    slots_held = lax.axis_size(RING)
    scal2 = jnp.stack([split, line]).astype(jnp.int32)

    x2 = lax.ppermute(inputs, "yh", SWAP)
    x1 = lax.ppermute(inputs, "c", SWAP)
    x3 = lax.ppermute(x2, "c", SWAP)
    up = [(i, i + 1) for i in range(shards - 1)]
    down = [(j, i) for i, j in up]
    before = lax.ppermute(keys_values[:, tokens - W :], SEQ, up)
    after = lax.ppermute(keys_values[:, :W], SEQ, down)

    weight_t = jnp.swapaxes(slot_weight.reshape(4, width, HEADS * R), 1, 2)
    kvh = call(
        prep_kernel,
        jax.ShapeDtypeStruct((HEADS, tokens, 2 * LANES), bf16),
        1, 8, 0, 2 << 20,
    )(scal, keys_values)

    slots = HEADS * R
    flops = 2 * tokens * slots * width
    acc_shape = jax.ShapeDtypeStruct((slots, tokens), f32)
    acc = call(partial_kernel, acc_shape, 3, 16, 2 * flops, 5 << 20)(
        scal, inputs, x1, weight_t
    )
    acc = call(more_kernel, acc_shape, 3, 16, flops, 6 << 20)(scal, x2, weight_t, acc)
    sent = pl.pallas_call(
        project_kernel,
        out_shape=jax.ShapeDtypeStruct((slots_held, 2 * ROWS, LANES), bf16),
        in_specs=[SMEM] + [VMEM] * 4,
        out_specs=pl.BlockSpec(memory_space=pltpu.HBM),
        scratch_shapes=[
            pltpu.VMEM((HEADS, R // ROWS, 2 * ROWS, LANES), bf16),
            pltpu.SemaphoreType.DMA((HEADS,)),
        ],
        compiler_params=pltpu.CompilerParams(vmem_limit_bytes=24 << 20),
        cost_estimate=pl.CostEstimate(
            flops=2 * flops, bytes_accessed=5 << 20, transcendentals=tokens * slots
        ),
    )(scal, x3, weight_t, acc, kvh)
    arrived = lax.all_to_all(sent, RING, 0, 0, tiled=True)

    near, stats, q2 = call(
        near_kernel,
        [
            jax.ShapeDtypeStruct((HEADS * DH, tokens), f32),
            jax.ShapeDtypeStruct((4 * HEADS, tokens), f32),
            jax.ShapeDtypeStruct((HEADS, tokens, LANES), bf16),
        ],
        4, 8, 4 * tokens * 3 * W * HEADS * LANES, 2 << 20, tokens * 3 * W * HEADS,
    )(scal, queries, keys_values, before, after)

    held = call(
        functools.partial(combine_kernel, lines, lax.axis_size("x"), tokens),
        jax.ShapeDtypeStruct((lines, 2 * ROWS, LANES), f32),
        1, 8, 0, 1 << 20, 1 << 17,
        scratch=[pltpu.VMEM((slots_held, ROWS, LANES), f32)],
    )(scal2, arrived)
    shared = lax.all_to_all(held, LINE, 0, 0, tiled=True)
    head = lax.div(slot * ROWS, R)
    gain = lax.dynamic_slice_in_dim(slot_gain, head * DH, DH, 1).reshape(1, 2 * DH)
    bias = lax.dynamic_slice_in_dim(slot_bias, head * DH, DH, 1).reshape(1, 2 * DH)
    chunk = call(
        norm_kernel,
        jax.ShapeDtypeStruct((slots_held, 2 * ROWS, LANES), bf16),
        3, 8, 0, 1 << 20, 1 << 15, 0,
    )(shared, gain, bias)
    table = lax.all_to_all(chunk, RING, 0, 0, tiled=True)

    return call(
        far_kernel,
        jax.ShapeDtypeStruct((tokens, HEADS * DH), bf16),
        4, 12, 4 * tokens * R * HEADS * LANES, 2 << 20, tokens * R * HEADS, 0,
    )(q2, table, near, stats)


def solution(mesh):
    finer = Mesh(mesh.devices.reshape(8, 4, 4, 2, 2), SEQ + DOC)
    return jax.shard_map(
        on_device,
        mesh=finer,
        in_specs=(
            P(SEQ, DOC),
            P(SEQ, DOC),
            P(None, SEQ, DOC),
            P(None, DOC),
            P(None, DOC),
            P(None, DOC),
            P(None, SEQ),
        ),
        out_specs=P(SEQ, DOC),
        check_vma=False,
    )
```

```python
import functools

import jax
import jax.numpy as jnp
from jax import lax
from jax.experimental import pallas as pl
from jax.experimental.pallas import tpu as pltpu
from jax.sharding import Mesh
from jax.sharding import PartitionSpec as P


DH = 64
R = 256
W = 128
HEADS = 4
LANES = 128
ROWS = 32
RING = ("z", "x")
LINE = "yl"
SEQ = ("z", "yl", "x")
DOC = ("yh", "c")
EPS = 1e-05
LOW = -1e30
SWAP = [(0, 1), (1, 0)]

f32 = jnp.float32
bf16 = jnp.bfloat16
VMEM = pl.BlockSpec(memory_space=pltpu.VMEM)
SMEM = pl.BlockSpec(memory_space=pltpu.SMEM)


def call(kernel, out_shape, n_in, vmem_mib, flops, nbytes, exps=0, scalars=1, scratch=()):
    single = not isinstance(out_shape, (list, tuple))
    return pl.pallas_call(
        kernel,
        out_shape=out_shape,
        in_specs=[SMEM] * scalars + [VMEM] * n_in,
        out_specs=VMEM if single else [VMEM] * len(out_shape),
        scratch_shapes=list(scratch),
        compiler_params=pltpu.CompilerParams(vmem_limit_bytes=vmem_mib << 20),
        cost_estimate=pl.CostEstimate(flops=flops, bytes_accessed=nbytes, transcendentals=exps),
    )


def dot_nt(a, b):
    return lax.dot_general(a, b, (((1,), (1,)), ((), ())), preferred_element_type=f32)


def dot_tn(a, b):
    return lax.dot_general(a, b, (((0,), (0,)), ((), ())), preferred_element_type=f32)


def lanes_of(shape):
    return lax.broadcasted_iota(jnp.int32, shape, len(shape) - 1)


def prep_kernel(scal, kv_ref, kvh_ref):
    tokens = kv_ref.shape[1]
    local = scal[0]
    second = lax.broadcasted_iota(jnp.int32, (tokens, LANES), 0) >= local
    left = lanes_of((tokens, LANES)) < DH
    for pair in range(HEADS // 2):
        cols = slice(pair * LANES, (pair + 1) * LANES)
        keys = kv_ref[0, :, cols].astype(f32)
        values = kv_ref[1, :, cols].astype(f32)
        keys_r = pltpu.roll(keys, DH, 1)
        values_r = pltpu.roll(values, DH, 1)
        for half in range(2):
            h = 2 * pair + half
            joined = jnp.where(left, keys, values_r) if half == 0 else jnp.where(left, keys_r, values)
            kvh_ref[h, :, :LANES] = jnp.where(second, 0.0, joined).astype(bf16)
            kvh_ref[h, :, LANES:] = jnp.where(second, joined, 0.0).astype(bf16)


def near_kernel(scal, q_ref, kv_ref, before_ref, after_ref, o_ref, stat_ref, q2_ref):
    tokens = q_ref.shape[0]
    local, base, total = scal[0], scal[1], scal[2]
    blocks = tokens // W
    span = 3 * W
    key = lax.broadcasted_iota(jnp.int32, (span, W), 0)
    query_at = lax.broadcasted_iota(jnp.int32, (span, W), 1)
    band = (key >= query_at) & (key - query_at <= 2 * W)
    left = lanes_of((W, LANES)) < DH
    place = lax.broadcasted_iota(jnp.int32, (W, LANES), 0)
    stat_ref[...] = jnp.zeros_like(stat_ref)

    def piece(s, at, cols):
        if at < 0:
            return before_ref[s, :, cols]
        if at >= blocks:
            return after_ref[s, :, cols]
        return kv_ref[s, at * W : (at + 1) * W, cols]

    for b in range(blocks):
        here = slice(b * W, (b + 1) * W)
        query_pos = query_at + b * W
        key_pos = key + (b - 1) * W
        allowed = (
            band
            & ((query_pos >= local) == (key_pos >= local))
            & (key_pos + base >= 0)
            & (key_pos + base < total)
        )
        second = place + b * W >= local
        stat_ref[HEADS : HEADS + 1, here] = jnp.where(query_pos[:1] >= local, 1.0, 0.0)
        for pair in range(HEADS // 2):
            cols = slice(pair * LANES, (pair + 1) * LANES)
            query = q_ref[here, cols].astype(f32) * 0.125
            query_r = pltpu.roll(query, DH, 1)
            keys = jnp.concatenate([piece(0, b + i, cols) for i in (-1, 0, 1)], axis=0)
            values = jnp.concatenate([piece(1, b + i, cols) for i in (-1, 0, 1)], axis=0)
            for half in range(2):
                h = 2 * pair + half
                both = jnp.where(left, query, query_r) if half == 0 else jnp.where(left, query_r, query)
                q2_ref[h, here] = jnp.where(left == second, 0.0, both).astype(bf16)
                mine = jnp.where(left if half == 0 else jnp.logical_not(left), query, 0.0).astype(bf16)
                scores = jnp.where(allowed, dot_nt(keys, mine), LOW)
                top = jnp.max(scores, axis=0, keepdims=True)
                weight = jnp.exp(scores - top)
                stat_ref[h : h + 1, here] = top
                stat_ref[2 * HEADS + h : 2 * HEADS + h + 1, here] = jnp.sum(
                    weight, axis=0, keepdims=True
                )
                out = dot_tn(values, weight.astype(bf16))
                o_ref[h * DH : (h + 1) * DH, here] = out[half * DH : (half + 1) * DH]


def pieces_of(top):
    a = top.astype(bf16).astype(f32)
    b = (top - a).astype(bf16).astype(f32)
    return a, b, top - a - b


def partial_kernel(scal, x0, x1, wt_ref, acc_ref):
    acc_ref[...] = dot_nt(wt_ref[scal[3]], x0[...]) + dot_nt(wt_ref[scal[4]], x1[...])


def more_kernel(scal, x2, wt_ref, acc_ref, out_ref):
    out_ref[...] = acc_ref[...] + dot_nt(wt_ref[scal[5]], x2[...])


def project_kernel(scal, x3, wt_ref, acc_ref, kvh_ref, out_ref, held, sems):
    tokens = x3.shape[0]
    local = scal[0]
    mixed = jnp.logical_and(local > 0, local < tokens)
    lane = lanes_of((R, LANES))
    at_a = lane == 0
    at_b = lane == DH
    left = lane < DH
    parts = R // ROWS

    def logits_of(h):
        rows = slice(h * R, (h + 1) * R)
        return acc_ref[rows, :] + dot_nt(wt_ref[scal[6], rows, :], x3[...])

    def from_first(n):
        return n - jnp.where(left, n[:, 0:1], n[:, DH : DH + 1])

    def put(h, hi, rest):
        packed = jnp.concatenate(
            [hi.reshape(parts, ROWS, LANES), rest.reshape(parts, ROWS, LANES)], axis=1
        )
        held[h] = packed.astype(bf16)
        copy = pltpu.make_async_copy(
            held.at[h], out_ref.at[pl.ds(h * parts, parts)], sems.at[h]
        )
        copy.start()
        return copy

    @pl.when(jnp.logical_not(mixed))
    def _():
        side = pl.multiple_of(jnp.where(local <= 0, LANES, 0), LANES)
        copies = []
        after = logits_of(0)
        for h in range(HEADS):
            logits = after
            if h + 1 < HEADS:
                after = logits_of(h + 1)
            a, b, c = pieces_of(jnp.max(logits, axis=1, keepdims=True))
            proj = jnp.exp(logits - (a + b)).astype(bf16)
            n = from_first(
                jnp.dot(proj, kvh_ref[h, :, pl.ds(side, LANES)], preferred_element_type=f32)
            )
            hi = n.astype(bf16).astype(f32)
            rest = jnp.where(at_a, c, jnp.where(at_b, 0.0, n - hi))
            hi = jnp.where(at_a, a, jnp.where(at_b, b, hi))
            copies.append(put(h, hi, rest))
        for copy in copies:
            copy.wait()

    @pl.when(mixed)
    def _():
        second = lax.broadcasted_iota(jnp.int32, (R, tokens), 1) >= local
        copies = []
        for h in range(HEADS):
            logits = logits_of(h)
            a0, b0, _ = pieces_of(jnp.max(jnp.where(second, LOW, logits), axis=1, keepdims=True))
            a1, b1, _ = pieces_of(jnp.max(jnp.where(second, logits, LOW), axis=1, keepdims=True))
            proj = jnp.exp(logits - jnp.where(second, a1 + b1, a0 + b0)).astype(bf16)
            sums = jnp.dot(proj, kvh_ref[h], preferred_element_type=f32)
            n0 = from_first(sums[:, :LANES])
            n1 = from_first(sums[:, LANES:])
            n0 = jnp.where(at_a, a0, jnp.where(at_b, b0, n0))
            n1 = jnp.where(at_a, a1, jnp.where(at_b, b1, n1))
            copies.append(put(h, n0, n1))
        for copy in copies:
            copy.wait()


def combine_kernel(lines, ring, tokens, scal, in_ref, out_ref, tops, held):
    senders = in_ref.shape[0]
    split, line = scal[0], scal[1]
    edge = lax.div(split, tokens)
    has_edge = jnp.logical_and(
        lax.rem(split, tokens) != 0, lax.rem(lax.div(edge, ring), lines) == line
    )
    slot = lax.div(edge, ring * lines) * ring + lax.rem(edge, ring)
    slot = jnp.where(has_edge, slot, 0)
    half = ROWS // 2
    shape = (half, LANES)
    low = jnp.full(shape, LOW, f32)
    border = jnp.full(shape, split - line * (ring * tokens), jnp.int32)
    lane = lanes_of(shape)
    starts = [((k // ring) * (ring * lines) + k % ring) * tokens for k in range(senders)]
    for part in range(2):
        hi = slice(part * half, (part + 1) * half)
        lo = slice(ROWS + part * half, ROWS + (part + 1) * half)
        extra = in_ref[slot, lo].astype(f32)
        extra_top = jnp.broadcast_to(extra[:, 0:1] + extra[:, DH : DH + 1], shape)
        extra_top = jnp.where(has_edge, extra_top, low)
        top0, full0, top1, full1 = low, low, extra_top, extra_top
        for k in range(senders):
            late = border <= starts[k]
            is_edge = jnp.logical_and(border > starts[k], border < starts[k] + tokens)
            first = in_ref[k, hi].astype(f32)
            other = jnp.where(is_edge, 0.0, in_ref[k, lo].astype(f32))
            top = jnp.broadcast_to(first[:, 0:1] + first[:, DH : DH + 1], shape)
            full = top + jnp.broadcast_to(other[:, 0:1], shape)
            tops[part, k] = top
            held[part, k] = first + other
            top0 = jnp.maximum(top0, jnp.where(late, low, top))
            full0 = jnp.maximum(full0, jnp.where(late, low, full))
            top1 = jnp.maximum(top1, jnp.where(late, top, low))
            full1 = jnp.maximum(full1, jnp.where(late, full, low))
        n0 = jnp.zeros(shape, f32)
        n1 = jnp.where(has_edge, extra * jnp.exp(extra_top - top1), 0.0)
        for k in range(senders):
            late = border <= starts[k]
            value = held[part, k] * jnp.exp(tops[part, k] - jnp.where(late, top1, top0))
            n0 = n0 + jnp.where(late, 0.0, value)
            n1 = n1 + jnp.where(late, value, 0.0)
        n0 = jnp.where(lane == 0, top0, jnp.where(lane == DH, full0, n0))
        n1 = jnp.where(lane == 0, top1, jnp.where(lane == DH, full1, n1))
        for line_at in range(lines):
            out_ref[line_at, hi] = n0
            out_ref[line_at, lo] = n1


def norm_kernel(in_ref, gain_ref, bias_ref, out_ref):
    got = in_ref[...]
    top = jnp.broadcast_to(got[:, :, 0:1], got.shape)
    whole = jnp.max(top, axis=0)
    full = jnp.max(jnp.broadcast_to(got[:, :, DH : DH + 1], got.shape), axis=0)
    n = jnp.sum(got * jnp.exp(top - whole[None]), axis=0)
    lane = lanes_of((2 * ROWS, LANES))
    left = lane < DH
    used = jnp.logical_and(lane != 0, lane != DH)

    def halves(v):
        a = jnp.sum(jnp.where(left, v, 0.0), axis=1, keepdims=True)
        b = jnp.sum(jnp.where(left, 0.0, v), axis=1, keepdims=True)
        return jnp.where(left, a, b) * (1.0 / DH)

    n = jnp.where(used, n, 0.0)
    centred = n - halves(n)
    variance = halves(centred * centred)
    scale = jnp.exp(2.0 * (full - whole))
    table = centred * lax.rsqrt(variance + EPS * scale) * gain_ref[...] + bias_ref[...]
    t0, t1 = table[:ROWS], table[ROWS:]
    left = left[:ROWS]
    keys = jnp.where(left, t0, pltpu.roll(t1, DH, 1))
    values = jnp.where(left, pltpu.roll(t0, DH, 1), t1)
    chunk = jnp.concatenate([keys, values], axis=0).astype(bf16)[None]
    out_ref[...] = jnp.broadcast_to(chunk, out_ref.shape)


def far_kernel(q2_ref, tab_ref, o_ref, stat_ref, out_ref):
    parts = R // ROWS
    second = stat_ref[HEADS : HEADS + 1, :] > 0.5

    def rows_of(h, part):
        return tab_ref[h * parts : (h + 1) * parts, part * ROWS : (part + 1) * ROWS].reshape(R, LANES)

    def scores_of(h):
        return dot_nt(rows_of(h, 0), q2_ref[h])

    after = scores_of(0)
    outs = []
    for h in range(HEADS):
        scores = after
        if h + 1 < HEADS:
            after = scores_of(h + 1)
        near_top = stat_ref[h : h + 1, :]
        near_total = stat_ref[2 * HEADS + h : 2 * HEADS + h + 1, :]
        top = jnp.maximum(jnp.max(scores, axis=0, keepdims=True), near_top)
        weight = jnp.exp(scores - top)
        scale = jnp.exp(near_top - top)
        total = jnp.sum(weight, axis=0, keepdims=True) + near_total * scale
        far = dot_tn(rows_of(h, 1), weight.astype(bf16))
        far = jnp.where(second, far[DH:], far[:DH])
        share = 1.0 / total
        outs.append(o_ref[h * DH : (h + 1) * DH] * (scale * share) + far * share)
        if h % 2 == 1:
            both = jnp.concatenate(outs, axis=0)
            outs = []
            at = (h // 2) * LANES
            out_ref[:, at : at + LANES] = jnp.transpose(both).astype(bf16)


def on_device(inputs, queries, keys_values, slot_weight, slot_gain, slot_bias, bounds):
    tokens, width = inputs.shape
    shards = lax.axis_size(SEQ)
    shard = lax.axis_index(SEQ)
    split = jnp.where(bounds[0, 0] > 0, bounds[0, 0], bounds[1, 0])
    base = shard * tokens
    yh, c = lax.axis_index("yh"), lax.axis_index("c")
    scal = jnp.stack(
        [
            split - base,
            base,
            jnp.int32(shards * tokens),
            yh * 2 + c,
            yh * 2 + 1 - c,
            (1 - yh) * 2 + c,
            (1 - yh) * 2 + 1 - c,
        ]
    ).astype(jnp.int32)
    line = lax.axis_index(LINE)
    slot = lax.axis_index(RING)
    lines = lax.axis_size(LINE)
    slots_held = lax.axis_size(RING)
    scal2 = jnp.stack([split, line]).astype(jnp.int32)

    x2 = lax.ppermute(inputs, "yh", SWAP)
    x1 = lax.ppermute(inputs, "c", SWAP)
    x3 = lax.ppermute(x2, "c", SWAP)
    up = [(i, i + 1) for i in range(shards - 1)]
    down = [(j, i) for i, j in up]
    before = lax.ppermute(keys_values[:, tokens - W :], SEQ, up)
    after = lax.ppermute(keys_values[:, :W], SEQ, down)

    weight_t = jnp.swapaxes(slot_weight.reshape(4, width, HEADS * R), 1, 2)
    kvh = call(
        prep_kernel,
        jax.ShapeDtypeStruct((HEADS, tokens, 2 * LANES), bf16),
        1, 8, 0, 2 << 20,
    )(scal, keys_values)

    slots = HEADS * R
    flops = 2 * tokens * slots * width
    acc_shape = jax.ShapeDtypeStruct((slots, tokens), f32)
    acc = call(partial_kernel, acc_shape, 3, 16, 2 * flops, 5 << 20)(
        scal, inputs, x1, weight_t
    )
    acc = call(more_kernel, acc_shape, 3, 16, flops, 6 << 20)(scal, x2, weight_t, acc)
    sent = pl.pallas_call(
        project_kernel,
        out_shape=jax.ShapeDtypeStruct((slots_held, 2 * ROWS, LANES), bf16),
        in_specs=[SMEM] + [VMEM] * 4,
        out_specs=pl.BlockSpec(memory_space=pltpu.HBM),
        scratch_shapes=[
            pltpu.VMEM((HEADS, R // ROWS, 2 * ROWS, LANES), bf16),
            pltpu.SemaphoreType.DMA((HEADS,)),
        ],
        compiler_params=pltpu.CompilerParams(vmem_limit_bytes=24 << 20),
        cost_estimate=pl.CostEstimate(
            flops=2 * flops, bytes_accessed=5 << 20, transcendentals=tokens * slots
        ),
    )(scal, x3, weight_t, acc, kvh)
    arrived = lax.all_to_all(sent, RING, 0, 0, tiled=True)

    near, stats, q2 = call(
        near_kernel,
        [
            jax.ShapeDtypeStruct((HEADS * DH, tokens), f32),
            jax.ShapeDtypeStruct((4 * HEADS, tokens), f32),
            jax.ShapeDtypeStruct((HEADS, tokens, LANES), bf16),
        ],
        4, 8, 4 * tokens * 3 * W * HEADS * LANES, 2 << 20, tokens * 3 * W * HEADS,
    )(scal, queries, keys_values, before, after)

    held = call(
        functools.partial(combine_kernel, lines, lax.axis_size("x"), tokens),
        jax.ShapeDtypeStruct((lines, 2 * ROWS, LANES), f32),
        1, 8, 0, 1 << 20, 1 << 17,
        scratch=[pltpu.VMEM((2, slots_held, ROWS // 2, LANES), f32)] * 2,
    )(scal2, arrived)
    shared = lax.all_to_all(held, LINE, 0, 0, tiled=True)
    head = lax.div(slot * ROWS, R)
    gain = lax.dynamic_slice_in_dim(slot_gain, head * DH, DH, 1).reshape(1, 2 * DH)
    bias = lax.dynamic_slice_in_dim(slot_bias, head * DH, DH, 1).reshape(1, 2 * DH)
    chunk = call(
        norm_kernel,
        jax.ShapeDtypeStruct((slots_held, 2 * ROWS, LANES), bf16),
        3, 8, 0, 1 << 20, 1 << 15, 0,
    )(shared, gain, bias)
    table = lax.all_to_all(chunk, RING, 0, 0, tiled=True)

    return call(
        far_kernel,
        jax.ShapeDtypeStruct((tokens, HEADS * DH), bf16),
        4, 12, 4 * tokens * R * HEADS * LANES, 2 << 20, tokens * R * HEADS, 0,
    )(q2, table, near, stats)


def solution(mesh):
    finer = Mesh(mesh.devices.reshape(8, 4, 4, 2, 2), SEQ + DOC)
    return jax.shard_map(
        on_device,
        mesh=finer,
        in_specs=(
            P(SEQ, DOC),
            P(SEQ, DOC),
            P(None, SEQ, DOC),
            P(None, DOC),
            P(None, DOC),
            P(None, DOC),
            P(None, SEQ),
        ),
        out_specs=P(SEQ, DOC),
        check_vma=False,
    )
```

```python
import functools

import jax
import jax.numpy as jnp
from jax import lax
from jax.experimental import pallas as pl
from jax.experimental.pallas import tpu as pltpu
from jax.sharding import Mesh
from jax.sharding import PartitionSpec as P


DH = 64
R = 256
W = 128
HEADS = 4
LANES = 128
ROWS = 32
RING = ("z", "x")
LINE = "yl"
SEQ = ("z", "yl", "x")
DOC = ("yh", "c")
EPS = 1e-05
LOW = -1e30
SWAP = [(0, 1), (1, 0)]

f32 = jnp.float32
bf16 = jnp.bfloat16
VMEM = pl.BlockSpec(memory_space=pltpu.VMEM)
SMEM = pl.BlockSpec(memory_space=pltpu.SMEM)


def call(kernel, out_shape, n_in, vmem_mib, flops, nbytes, exps=0, scalars=1, scratch=()):
    single = not isinstance(out_shape, (list, tuple))
    return pl.pallas_call(
        kernel,
        out_shape=out_shape,
        in_specs=[SMEM] * scalars + [VMEM] * n_in,
        out_specs=VMEM if single else [VMEM] * len(out_shape),
        scratch_shapes=list(scratch),
        compiler_params=pltpu.CompilerParams(vmem_limit_bytes=vmem_mib << 20),
        cost_estimate=pl.CostEstimate(flops=flops, bytes_accessed=nbytes, transcendentals=exps),
    )


def dot_nt(a, b):
    return lax.dot_general(a, b, (((1,), (1,)), ((), ())), preferred_element_type=f32)


def dot_nn(a, b):
    return jnp.dot(a, b, preferred_element_type=f32)


def dot_tn(a, b):
    return lax.dot_general(a, b, (((0,), (0,)), ((), ())), preferred_element_type=f32)


def lanes_of(shape):
    return lax.broadcasted_iota(jnp.int32, shape, len(shape) - 1)


def prep_kernel(scal, kv_ref, kvh_ref):
    tokens = kv_ref.shape[1]
    local = scal[0]
    second = lax.broadcasted_iota(jnp.int32, (tokens, LANES), 0) >= local
    left = lanes_of((tokens, LANES)) < DH
    for pair in range(HEADS // 2):
        cols = slice(pair * LANES, (pair + 1) * LANES)
        keys = kv_ref[0, :, cols].astype(f32)
        values = kv_ref[1, :, cols].astype(f32)
        keys_r = pltpu.roll(keys, DH, 1)
        values_r = pltpu.roll(values, DH, 1)
        for half in range(2):
            h = 2 * pair + half
            joined = jnp.where(left, keys, values_r) if half == 0 else jnp.where(left, keys_r, values)
            kvh_ref[h, :, :LANES] = jnp.where(second, 0.0, joined).astype(bf16)
            kvh_ref[h, :, LANES:] = jnp.where(second, joined, 0.0).astype(bf16)


def near_kernel(scal, q_ref, kv_ref, before_ref, after_ref, o_ref, stat_ref, q2_ref):
    tokens = q_ref.shape[0]
    local, base, total = scal[0], scal[1], scal[2]
    blocks = tokens // W
    span = 3 * W
    key = lax.broadcasted_iota(jnp.int32, (span, W), 0)
    query_at = lax.broadcasted_iota(jnp.int32, (span, W), 1)
    band = (key >= query_at) & (key - query_at <= 2 * W)
    left = lanes_of((W, LANES)) < DH
    place = lax.broadcasted_iota(jnp.int32, (W, LANES), 0)
    stat_ref[...] = jnp.zeros_like(stat_ref)

    def piece(s, at, cols):
        if at < 0:
            return before_ref[s, :, cols]
        if at >= blocks:
            return after_ref[s, :, cols]
        return kv_ref[s, at * W : (at + 1) * W, cols]

    for b in range(blocks):
        here = slice(b * W, (b + 1) * W)
        query_pos = query_at + b * W
        key_pos = key + (b - 1) * W
        allowed = (
            band
            & ((query_pos >= local) == (key_pos >= local))
            & (key_pos + base >= 0)
            & (key_pos + base < total)
        )
        second = place + b * W >= local
        stat_ref[HEADS : HEADS + 1, here] = jnp.where(query_pos[:1] >= local, 1.0, 0.0)
        for pair in range(HEADS // 2):
            cols = slice(pair * LANES, (pair + 1) * LANES)
            query = q_ref[here, cols].astype(f32) * 0.125
            query_r = pltpu.roll(query, DH, 1)
            keys = jnp.concatenate([piece(0, b + i, cols) for i in (-1, 0, 1)], axis=0)
            values = jnp.concatenate([piece(1, b + i, cols) for i in (-1, 0, 1)], axis=0)
            for half in range(2):
                h = 2 * pair + half
                both = jnp.where(left, query, query_r) if half == 0 else jnp.where(left, query_r, query)
                q2_ref[h, here] = jnp.where(left == second, 0.0, both).astype(bf16)
                mine = jnp.where(left if half == 0 else jnp.logical_not(left), query, 0.0).astype(bf16)
                scores = jnp.where(allowed, dot_nt(keys, mine), LOW)
                top = jnp.max(scores, axis=0, keepdims=True)
                weight = jnp.exp(scores - top)
                stat_ref[h : h + 1, here] = top
                stat_ref[2 * HEADS + h : 2 * HEADS + h + 1, here] = jnp.sum(
                    weight, axis=0, keepdims=True
                )
                out = dot_tn(values, weight.astype(bf16))
                o_ref[h * DH : (h + 1) * DH, here] = out[half * DH : (half + 1) * DH]


def pieces_of(top):
    a = top.astype(bf16).astype(f32)
    b = (top - a).astype(bf16).astype(f32)
    return a, b, top - a - b


def partial_kernel(scal, x0, x1, wt_ref, acc_ref):
    acc_ref[...] = dot_nt(wt_ref[scal[3]], x0[...]) + dot_nt(wt_ref[scal[4]], x1[...])


def more_kernel(scal, x2, wt_ref, acc_ref, out_ref):
    out_ref[...] = acc_ref[...] + dot_nt(wt_ref[scal[5]], x2[...])


def project_kernel(scal, x3, wt_ref, acc_ref, kvh_ref, out_ref, held, sems):
    tokens = x3.shape[0]
    local = scal[0]
    mixed = jnp.logical_and(local > 0, local < tokens)
    lane = lanes_of((R, LANES))
    at_a = lane == 0
    at_b = lane == DH
    left = lane < DH
    parts = R // ROWS

    def logits_of(h):
        rows = slice(h * R, (h + 1) * R)
        return acc_ref[rows, :] + dot_nt(wt_ref[scal[6], rows, :], x3[...])

    def from_first(n):
        return n - jnp.where(left, n[:, 0:1], n[:, DH : DH + 1])

    def put(h, hi, rest):
        packed = jnp.concatenate(
            [hi.reshape(parts, ROWS, LANES), rest.reshape(parts, ROWS, LANES)], axis=1
        )
        held[h] = packed.astype(bf16)
        copy = pltpu.make_async_copy(
            held.at[h], out_ref.at[pl.ds(h * parts, parts)], sems.at[h]
        )
        copy.start()
        return copy

    @pl.when(jnp.logical_not(mixed))
    def _():
        side = pl.multiple_of(jnp.where(local <= 0, LANES, 0), LANES)
        copies = []
        after = logits_of(0)
        for h in range(HEADS):
            logits = after
            if h + 1 < HEADS:
                after = logits_of(h + 1)
            a, b, c = pieces_of(jnp.max(logits, axis=1, keepdims=True))
            proj = jnp.exp(logits - (a + b)).astype(bf16)
            n = from_first(
                jnp.dot(proj, kvh_ref[h, :, pl.ds(side, LANES)], preferred_element_type=f32)
            )
            hi = n.astype(bf16).astype(f32)
            rest = jnp.where(at_a, c, jnp.where(at_b, 0.0, n - hi))
            hi = jnp.where(at_a, a, jnp.where(at_b, b, hi))
            copies.append(put(h, hi, rest))
        for copy in copies:
            copy.wait()

    @pl.when(mixed)
    def _():
        second = lax.broadcasted_iota(jnp.int32, (R, tokens), 1) >= local
        copies = []
        for h in range(HEADS):
            logits = logits_of(h)
            a0, b0, _ = pieces_of(jnp.max(jnp.where(second, LOW, logits), axis=1, keepdims=True))
            a1, b1, _ = pieces_of(jnp.max(jnp.where(second, logits, LOW), axis=1, keepdims=True))
            proj = jnp.exp(logits - jnp.where(second, a1 + b1, a0 + b0)).astype(bf16)
            sums = jnp.dot(proj, kvh_ref[h], preferred_element_type=f32)
            n0 = from_first(sums[:, :LANES])
            n1 = from_first(sums[:, LANES:])
            n0 = jnp.where(at_a, a0, jnp.where(at_b, b0, n0))
            n1 = jnp.where(at_a, a1, jnp.where(at_b, b1, n1))
            copies.append(put(h, n0, n1))
        for copy in copies:
            copy.wait()


def combine_kernel(lines, ring, tokens, scal, in_ref, out_ref, tops, fine):
    senders = in_ref.shape[0]
    slot = scal[1]
    has_edge = scal[2] > 0
    shape = (ROWS, LANES)
    flat = (senders * ROWS, LANES)
    row = lax.broadcasted_iota(jnp.int32, (LANES, LANES), 0)
    pick_both = jnp.where((row == 0) | (row == DH), 1.0, 0.0).astype(bf16)
    pick_first = jnp.where(row == 0, 1.0, 0.0).astype(bf16)
    tops[...] = dot_nn(in_ref[:, :ROWS].reshape(flat), pick_both).reshape(tops.shape)
    fine[...] = dot_nn(in_ref[:, ROWS:].reshape(flat), pick_first).reshape(fine.shape)
    low = jnp.full(shape, LOW, f32)
    border = jnp.full(shape, scal[0], jnp.int32)
    starts = [((k // ring) * (ring * lines) + k % ring) * tokens for k in range(senders)]
    extra = in_ref[slot, ROWS:]
    extra_top = jnp.where(has_edge, dot_nn(extra, pick_both), low)
    top0, full0, top1, full1 = low, low, extra_top, extra_top
    for k in range(senders):
        late = border <= starts[k]
        is_edge = jnp.logical_and(border > starts[k], border < starts[k] + tokens)
        top = tops[k]
        full = top + jnp.where(is_edge, 0.0, fine[k])
        top0 = jnp.maximum(top0, jnp.where(late, low, top))
        full0 = jnp.maximum(full0, jnp.where(late, low, full))
        top1 = jnp.maximum(top1, jnp.where(late, top, low))
        full1 = jnp.maximum(full1, jnp.where(late, full, low))
    n0 = jnp.zeros(shape, f32)
    n1 = jnp.where(has_edge, extra.astype(f32) * jnp.exp(extra_top - top1), 0.0)
    for k in range(senders):
        late = border <= starts[k]
        is_edge = jnp.logical_and(border > starts[k], border < starts[k] + tokens)
        value = in_ref[k, :ROWS].astype(f32) + jnp.where(is_edge, 0.0, in_ref[k, ROWS:].astype(f32))
        value = value * jnp.exp(tops[k] - jnp.where(late, top1, top0))
        n0 = n0 + jnp.where(late, 0.0, value)
        n1 = n1 + jnp.where(late, value, 0.0)
    lane = lanes_of(shape)
    n0 = jnp.where(lane == 0, top0, jnp.where(lane == DH, full0, n0))
    n1 = jnp.where(lane == 0, top1, jnp.where(lane == DH, full1, n1))
    for at in range(lines):
        out_ref[at, :ROWS] = n0
        out_ref[at, ROWS:] = n1


def norm_kernel(in_ref, gain_ref, bias_ref, out_ref):
    got = in_ref[...]
    top = jnp.broadcast_to(got[:, :, 0:1], got.shape)
    whole = jnp.max(top, axis=0)
    full = jnp.max(jnp.broadcast_to(got[:, :, DH : DH + 1], got.shape), axis=0)
    n = jnp.sum(got * jnp.exp(top - whole[None]), axis=0)
    lane = lanes_of((2 * ROWS, LANES))
    left = lane < DH
    used = jnp.logical_and(lane != 0, lane != DH)

    def halves(v):
        a = jnp.sum(jnp.where(left, v, 0.0), axis=1, keepdims=True)
        b = jnp.sum(jnp.where(left, 0.0, v), axis=1, keepdims=True)
        return jnp.where(left, a, b) * (1.0 / DH)

    n = jnp.where(used, n, 0.0)
    centred = n - halves(n)
    variance = halves(centred * centred)
    scale = jnp.exp(2.0 * (full - whole))
    table = centred * lax.rsqrt(variance + EPS * scale) * gain_ref[...] + bias_ref[...]
    t0, t1 = table[:ROWS], table[ROWS:]
    left = left[:ROWS]
    keys = jnp.where(left, t0, pltpu.roll(t1, DH, 1))
    values = jnp.where(left, pltpu.roll(t0, DH, 1), t1)
    chunk = jnp.concatenate([keys, values], axis=0).astype(bf16)[None]
    out_ref[...] = jnp.broadcast_to(chunk, out_ref.shape)


def far_kernel(q2_ref, tab_ref, o_ref, stat_ref, out_ref):
    parts = R // ROWS
    second = stat_ref[HEADS : HEADS + 1, :] > 0.5

    def rows_of(h, part):
        return tab_ref[h * parts : (h + 1) * parts, part * ROWS : (part + 1) * ROWS].reshape(R, LANES)

    def scores_of(h):
        return dot_nt(rows_of(h, 0), q2_ref[h])

    after = scores_of(0)
    outs = []
    for h in range(HEADS):
        scores = after
        if h + 1 < HEADS:
            after = scores_of(h + 1)
        near_top = stat_ref[h : h + 1, :]
        near_total = stat_ref[2 * HEADS + h : 2 * HEADS + h + 1, :]
        top = jnp.maximum(jnp.max(scores, axis=0, keepdims=True), near_top)
        weight = jnp.exp(scores - top)
        scale = jnp.exp(near_top - top)
        total = jnp.sum(weight, axis=0, keepdims=True) + near_total * scale
        far = dot_tn(rows_of(h, 1), weight.astype(bf16))
        far = jnp.where(second, far[DH:], far[:DH])
        share = 1.0 / total
        outs.append(o_ref[h * DH : (h + 1) * DH] * (scale * share) + far * share)
        if h % 2 == 1:
            both = jnp.concatenate(outs, axis=0)
            outs = []
            at = (h // 2) * LANES
            out_ref[:, at : at + LANES] = jnp.transpose(both).astype(bf16)


def on_device(inputs, queries, keys_values, slot_weight, slot_gain, slot_bias, bounds):
    tokens, width = inputs.shape
    shards = lax.axis_size(SEQ)
    shard = lax.axis_index(SEQ)
    split = jnp.where(bounds[0, 0] > 0, bounds[0, 0], bounds[1, 0])
    base = shard * tokens
    yh, c = lax.axis_index("yh"), lax.axis_index("c")
    scal = jnp.stack(
        [
            split - base,
            base,
            jnp.int32(shards * tokens),
            yh * 2 + c,
            yh * 2 + 1 - c,
            (1 - yh) * 2 + c,
            (1 - yh) * 2 + 1 - c,
        ]
    ).astype(jnp.int32)
    line = lax.axis_index(LINE)
    slot = lax.axis_index(RING)
    lines = lax.axis_size(LINE)
    slots_held = lax.axis_size(RING)
    ring = lax.axis_size("x")
    edge = split // tokens
    has_edge = (split % tokens != 0) & ((edge // ring) % lines == line)
    edge_slot = jnp.where(has_edge, edge // (ring * lines) * ring + edge % ring, 0)
    scal2 = jnp.stack([split - line * (ring * tokens), edge_slot, has_edge]).astype(jnp.int32)

    x2 = lax.ppermute(inputs, "yh", SWAP)
    x1 = lax.ppermute(inputs, "c", SWAP)
    x3 = lax.ppermute(x2, "c", SWAP)
    up = [(i, i + 1) for i in range(shards - 1)]
    down = [(j, i) for i, j in up]
    before = lax.ppermute(keys_values[:, tokens - W :], SEQ, up)
    after = lax.ppermute(keys_values[:, :W], SEQ, down)

    weight_t = jnp.swapaxes(slot_weight.reshape(4, width, HEADS * R), 1, 2)
    kvh = call(
        prep_kernel,
        jax.ShapeDtypeStruct((HEADS, tokens, 2 * LANES), bf16),
        1, 8, 0, 2 << 20,
    )(scal, keys_values)

    slots = HEADS * R
    flops = 2 * tokens * slots * width
    acc_shape = jax.ShapeDtypeStruct((slots, tokens), f32)
    acc = call(partial_kernel, acc_shape, 3, 16, 2 * flops, 5 << 20)(
        scal, inputs, x1, weight_t
    )
    acc = call(more_kernel, acc_shape, 3, 16, flops, 6 << 20)(scal, x2, weight_t, acc)
    sent = pl.pallas_call(
        project_kernel,
        out_shape=jax.ShapeDtypeStruct((slots_held, 2 * ROWS, LANES), bf16),
        in_specs=[SMEM] + [VMEM] * 4,
        out_specs=pl.BlockSpec(memory_space=pltpu.HBM),
        scratch_shapes=[
            pltpu.VMEM((HEADS, R // ROWS, 2 * ROWS, LANES), bf16),
            pltpu.SemaphoreType.DMA((HEADS,)),
        ],
        compiler_params=pltpu.CompilerParams(vmem_limit_bytes=24 << 20),
        cost_estimate=pl.CostEstimate(
            flops=2 * flops, bytes_accessed=5 << 20, transcendentals=tokens * slots
        ),
    )(scal, x3, weight_t, acc, kvh)
    arrived = lax.all_to_all(sent, RING, 0, 0, tiled=True)

    near, stats, q2 = call(
        near_kernel,
        [
            jax.ShapeDtypeStruct((HEADS * DH, tokens), f32),
            jax.ShapeDtypeStruct((4 * HEADS, tokens), f32),
            jax.ShapeDtypeStruct((HEADS, tokens, LANES), bf16),
        ],
        4, 8, 4 * tokens * 3 * W * HEADS * LANES, 2 << 20, tokens * 3 * W * HEADS,
    )(scal, queries, keys_values, before, after)

    held = call(
        functools.partial(combine_kernel, lines, lax.axis_size("x"), tokens),
        jax.ShapeDtypeStruct((lines, 2 * ROWS, LANES), f32),
        1, 8, 0, 1 << 20, 1 << 17,
        scratch=[pltpu.VMEM((slots_held, ROWS, LANES), f32)] * 2,
    )(scal2, arrived)
    shared = lax.all_to_all(held, LINE, 0, 0, tiled=True)
    head = lax.div(slot * ROWS, R)
    gain = lax.dynamic_slice_in_dim(slot_gain, head * DH, DH, 1).reshape(1, 2 * DH)
    bias = lax.dynamic_slice_in_dim(slot_bias, head * DH, DH, 1).reshape(1, 2 * DH)
    chunk = call(
        norm_kernel,
        jax.ShapeDtypeStruct((slots_held, 2 * ROWS, LANES), bf16),
        3, 8, 0, 1 << 20, 1 << 15, 0,
    )(shared, gain, bias)
    table = lax.all_to_all(chunk, RING, 0, 0, tiled=True)

    return call(
        far_kernel,
        jax.ShapeDtypeStruct((tokens, HEADS * DH), bf16),
        4, 12, 4 * tokens * R * HEADS * LANES, 2 << 20, tokens * R * HEADS, 0,
    )(q2, table, near, stats)


def solution(mesh):
    finer = Mesh(mesh.devices.reshape(8, 4, 4, 2, 2), SEQ + DOC)
    return jax.shard_map(
        on_device,
        mesh=finer,
        in_specs=(
            P(SEQ, DOC),
            P(SEQ, DOC),
            P(None, SEQ, DOC),
            P(None, DOC),
            P(None, DOC),
            P(None, DOC),
            P(None, SEQ),
        ),
        out_specs=P(SEQ, DOC),
        check_vma=False,
    )
```

```python
import functools

import jax
import jax.numpy as jnp
from jax import lax
from jax.experimental import pallas as pl
from jax.experimental.pallas import tpu as pltpu
from jax.sharding import Mesh
from jax.sharding import PartitionSpec as P


DH = 64
R = 256
W = 128
HEADS = 4
LANES = 128
GROUP = 4
GATHER = (("z", "yl"),)
SHARE = ("x",)
SEQ = ("z", "yl", "x")
DOC = ("yh", "c")
EPS = 1e-05
LOW = -1e30
SWAP = [(0, 1), (1, 0)]

f32 = jnp.float32
bf16 = jnp.bfloat16
VMEM = pl.BlockSpec(memory_space=pltpu.VMEM)
SMEM = pl.BlockSpec(memory_space=pltpu.SMEM)


def call(kernel, out_shape, n_in, vmem_mib, flops, nbytes, exps=0, scalars=1, scratch=()):
    single = not isinstance(out_shape, (list, tuple))
    return pl.pallas_call(
        kernel,
        out_shape=out_shape,
        in_specs=[SMEM] * scalars + [VMEM] * n_in,
        out_specs=VMEM if single else [VMEM] * len(out_shape),
        scratch_shapes=list(scratch),
        compiler_params=pltpu.CompilerParams(vmem_limit_bytes=vmem_mib << 20),
        cost_estimate=pl.CostEstimate(flops=flops, bytes_accessed=nbytes, transcendentals=exps),
    )


def dot_nt(a, b):
    return lax.dot_general(a, b, (((1,), (1,)), ((), ())), preferred_element_type=f32)


def dot_nn(a, b):
    return jnp.dot(a, b, preferred_element_type=f32)


def dot_tn(a, b):
    return lax.dot_general(a, b, (((0,), (0,)), ((), ())), preferred_element_type=f32)


def lanes_of(shape):
    return lax.broadcasted_iota(jnp.int32, shape, len(shape) - 1)


def prep_kernel(scal, kv_ref, kvh_ref):
    tokens = kv_ref.shape[1]
    local = scal[0]
    second = lax.broadcasted_iota(jnp.int32, (tokens, LANES), 0) >= local
    left = lanes_of((tokens, LANES)) < DH
    for pair in range(HEADS // 2):
        cols = slice(pair * LANES, (pair + 1) * LANES)
        keys = kv_ref[0, :, cols].astype(f32)
        values = kv_ref[1, :, cols].astype(f32)
        keys_r = pltpu.roll(keys, DH, 1)
        values_r = pltpu.roll(values, DH, 1)
        for half in range(2):
            h = 2 * pair + half
            joined = jnp.where(left, keys, values_r) if half == 0 else jnp.where(left, keys_r, values)
            kvh_ref[h, :, :LANES] = jnp.where(second, 0.0, joined).astype(bf16)
            kvh_ref[h, :, LANES:] = jnp.where(second, joined, 0.0).astype(bf16)


def near_kernel(scal, q_ref, kv_ref, before_ref, after_ref, o_ref, stat_ref, q2_ref):
    tokens = q_ref.shape[0]
    local, base, total = scal[0], scal[1], scal[2]
    blocks = tokens // W
    span = 3 * W
    key = lax.broadcasted_iota(jnp.int32, (span, W), 0)
    query_at = lax.broadcasted_iota(jnp.int32, (span, W), 1)
    band = (key >= query_at) & (key - query_at <= 2 * W)
    left = lanes_of((W, LANES)) < DH
    place = lax.broadcasted_iota(jnp.int32, (W, LANES), 0)
    stat_ref[...] = jnp.zeros_like(stat_ref)

    def piece(s, at, cols):
        if at < 0:
            return before_ref[s, :, cols]
        if at >= blocks:
            return after_ref[s, :, cols]
        return kv_ref[s, at * W : (at + 1) * W, cols]

    for b in range(blocks):
        here = slice(b * W, (b + 1) * W)
        query_pos = query_at + b * W
        key_pos = key + (b - 1) * W
        allowed = (
            band
            & ((query_pos >= local) == (key_pos >= local))
            & (key_pos + base >= 0)
            & (key_pos + base < total)
        )
        second = place + b * W >= local
        stat_ref[HEADS : HEADS + 1, here] = jnp.where(query_pos[:1] >= local, 1.0, 0.0)
        for pair in range(HEADS // 2):
            cols = slice(pair * LANES, (pair + 1) * LANES)
            query = q_ref[here, cols].astype(f32) * 0.125
            query_r = pltpu.roll(query, DH, 1)
            keys = jnp.concatenate([piece(0, b + i, cols) for i in (-1, 0, 1)], axis=0)
            values = jnp.concatenate([piece(1, b + i, cols) for i in (-1, 0, 1)], axis=0)
            for half in range(2):
                h = 2 * pair + half
                both = jnp.where(left, query, query_r) if half == 0 else jnp.where(left, query_r, query)
                q2_ref[h, here] = jnp.where(left == second, 0.0, both).astype(bf16)
                mine = jnp.where(left if half == 0 else jnp.logical_not(left), query, 0.0).astype(bf16)
                scores = jnp.where(allowed, dot_nt(keys, mine), LOW)
                top = jnp.max(scores, axis=0, keepdims=True)
                weight = jnp.exp(scores - top)
                stat_ref[h : h + 1, here] = top
                stat_ref[2 * HEADS + h : 2 * HEADS + h + 1, here] = jnp.sum(
                    weight, axis=0, keepdims=True
                )
                out = dot_tn(values, weight.astype(bf16))
                o_ref[h * DH : (h + 1) * DH, here] = out[half * DH : (half + 1) * DH]


def pieces_of(top):
    a = top.astype(bf16).astype(f32)
    b = (top - a).astype(bf16).astype(f32)
    return a, b, top - a - b


def partial_kernel(scal, x0, x1, wt_ref, acc_ref):
    acc_ref[...] = dot_nt(wt_ref[scal[3]], x0[...]) + dot_nt(wt_ref[scal[4]], x1[...])


def more_kernel(scal, x2, wt_ref, acc_ref, out_ref):
    out_ref[...] = acc_ref[...] + dot_nt(wt_ref[scal[5]], x2[...])


def project_kernel(group, count, scal, x3, wt_ref, acc_ref, kvh_ref, out_ref, held, sems):
    tokens = x3.shape[0]
    local = scal[0]
    mixed = jnp.logical_and(local > 0, local < tokens)
    lane = lanes_of((R, LANES))
    at_a = lane == 0
    at_b = lane == DH
    left = lane < DH
    parts = R // count

    def logits_of(i):
        at = (group * GROUP + i) * R
        rows = slice(at, at + R)
        return acc_ref[rows, :] + dot_nt(wt_ref[scal[6], rows, :], x3[...])

    def from_first(n):
        return n - jnp.where(left, n[:, 0:1], n[:, DH : DH + 1])

    def put(i, hi, rest):
        packed = jnp.concatenate(
            [hi.reshape(parts, count, LANES), rest.reshape(parts, count, LANES)], axis=1
        )
        held[i] = packed.astype(bf16)
        copy = pltpu.make_async_copy(
            held.at[i], out_ref.at[pl.ds(i * parts, parts)], sems.at[i]
        )
        copy.start()
        return copy

    @pl.when(jnp.logical_not(mixed))
    def _():
        side = pl.multiple_of(jnp.where(local <= 0, LANES, 0), LANES)
        copies = []
        after = logits_of(0)
        for i in range(GROUP):
            h = group * GROUP + i
            logits = after
            if i + 1 < GROUP:
                after = logits_of(i + 1)
            a, b, c = pieces_of(jnp.max(logits, axis=1, keepdims=True))
            proj = jnp.exp(logits - (a + b)).astype(bf16)
            n = from_first(dot_nn(proj, kvh_ref[h, :, pl.ds(side, LANES)]))
            hi = n.astype(bf16).astype(f32)
            rest = jnp.where(at_a, c, jnp.where(at_b, 0.0, n - hi))
            hi = jnp.where(at_a, a, jnp.where(at_b, b, hi))
            copies.append(put(i, hi, rest))
        for copy in copies:
            copy.wait()

    @pl.when(mixed)
    def _():
        second = lax.broadcasted_iota(jnp.int32, (R, tokens), 1) >= local
        copies = []
        for i in range(GROUP):
            h = group * GROUP + i
            logits = logits_of(i)
            a0, b0, _ = pieces_of(jnp.max(jnp.where(second, LOW, logits), axis=1, keepdims=True))
            a1, b1, _ = pieces_of(jnp.max(jnp.where(second, logits, LOW), axis=1, keepdims=True))
            proj = jnp.exp(logits - jnp.where(second, a1 + b1, a0 + b0)).astype(bf16)
            sums = dot_nn(proj, kvh_ref[h])
            n0 = from_first(sums[:, :LANES])
            n1 = from_first(sums[:, LANES:])
            n0 = jnp.where(at_a, a0, jnp.where(at_b, b0, n0))
            n1 = jnp.where(at_a, a1, jnp.where(at_b, b1, n1))
            copies.append(put(i, n0, n1))
        for copy in copies:
            copy.wait()


def combine_kernel(starts, tokens, count, scal, in_ref, out_ref, tops, fine):
    senders = in_ref.shape[0]
    slot = scal[1]
    has_edge = scal[2] > 0
    shape = (count, LANES)
    flat = (senders * count, LANES)
    row = lax.broadcasted_iota(jnp.int32, (LANES, LANES), 0)
    pick_both = jnp.where((row == 0) | (row == DH), 1.0, 0.0).astype(bf16)
    pick_first = jnp.where(row == 0, 1.0, 0.0).astype(bf16)
    tops[...] = dot_nn(in_ref[:, :count].reshape(flat), pick_both).reshape(tops.shape)
    fine[...] = dot_nn(in_ref[:, count:].reshape(flat), pick_first).reshape(fine.shape)
    low = jnp.full(shape, LOW, f32)
    border = jnp.full(shape, scal[0], jnp.int32)
    extra = in_ref[slot, count:]
    extra_top = jnp.where(has_edge, dot_nn(extra, pick_both), low)
    top0, full0, top1, full1 = low, low, extra_top, extra_top
    for k in range(senders):
        late = border <= starts[k]
        is_edge = jnp.logical_and(border > starts[k], border < starts[k] + tokens)
        top = tops[k]
        full = top + jnp.where(is_edge, 0.0, fine[k])
        top0 = jnp.maximum(top0, jnp.where(late, low, top))
        full0 = jnp.maximum(full0, jnp.where(late, low, full))
        top1 = jnp.maximum(top1, jnp.where(late, top, low))
        full1 = jnp.maximum(full1, jnp.where(late, full, low))
    n0 = jnp.zeros(shape, f32)
    n1 = jnp.where(has_edge, extra.astype(f32) * jnp.exp(extra_top - top1), 0.0)
    for k in range(senders):
        late = border <= starts[k]
        is_edge = jnp.logical_and(border > starts[k], border < starts[k] + tokens)
        value = in_ref[k, :count].astype(f32) + jnp.where(is_edge, 0.0, in_ref[k, count:].astype(f32))
        value = value * jnp.exp(tops[k] - jnp.where(late, top1, top0))
        n0 = n0 + jnp.where(late, 0.0, value)
        n1 = n1 + jnp.where(late, value, 0.0)
    lane = lanes_of(shape)
    n0 = jnp.where(lane == 0, top0, jnp.where(lane == DH, full0, n0))
    n1 = jnp.where(lane == 0, top1, jnp.where(lane == DH, full1, n1))
    for at in range(out_ref.shape[0]):
        out_ref[at, :count] = n0
        out_ref[at, count:] = n1


def norm_kernel(in_ref, gain_ref, bias_ref, out_ref):
    count = in_ref.shape[1] // 2
    got = in_ref[...]
    top = jnp.broadcast_to(got[:, :, 0:1], got.shape)
    whole = jnp.max(top, axis=0)
    full = jnp.max(jnp.broadcast_to(got[:, :, DH : DH + 1], got.shape), axis=0)
    n = jnp.sum(got * jnp.exp(top - whole[None]), axis=0)
    lane = lanes_of((2 * count, LANES))
    left = lane < DH
    used = jnp.logical_and(lane != 0, lane != DH)

    def halves(v):
        a = jnp.sum(jnp.where(left, v, 0.0), axis=1, keepdims=True)
        b = jnp.sum(jnp.where(left, 0.0, v), axis=1, keepdims=True)
        return jnp.where(left, a, b) * (1.0 / DH)

    n = jnp.where(used, n, 0.0)
    centred = n - halves(n)
    variance = halves(centred * centred)
    scale = jnp.exp(2.0 * (full - whole))
    table = centred * lax.rsqrt(variance + EPS * scale) * gain_ref[...] + bias_ref[...]
    t0, t1 = table[:count], table[count:]
    left = left[:count]
    keys = jnp.where(left, t0, pltpu.roll(t1, DH, 1))
    values = jnp.where(left, pltpu.roll(t0, DH, 1), t1)
    chunk = jnp.concatenate([keys, values], axis=0).astype(bf16)[None]
    out_ref[...] = jnp.broadcast_to(chunk, out_ref.shape)


def far_kernel(group, q2_ref, tab_ref, o_ref, stat_ref, *rest):
    out_ref = rest[-1]
    count = tab_ref.shape[1] // 2
    parts = R // count
    second = stat_ref[HEADS : HEADS + 1, :] > 0.5
    for i, done in enumerate(rest[:-1]):
        out_ref[:, i * LANES : (i + 1) * LANES] = done[...]

    def rows_of(i, part):
        return tab_ref[
            i * parts : (i + 1) * parts, part * count : (part + 1) * count
        ].reshape(R, LANES)

    def scores_of(i):
        return dot_nt(rows_of(i, 0), q2_ref[group * GROUP + i])

    after = scores_of(0)
    outs = []
    for i in range(GROUP):
        h = group * GROUP + i
        scores = after
        if i + 1 < GROUP:
            after = scores_of(i + 1)
        near_top = stat_ref[h : h + 1, :]
        near_total = stat_ref[2 * HEADS + h : 2 * HEADS + h + 1, :]
        top = jnp.maximum(jnp.max(scores, axis=0, keepdims=True), near_top)
        weight = jnp.exp(scores - top)
        scale = jnp.exp(near_top - top)
        total = jnp.sum(weight, axis=0, keepdims=True) + near_total * scale
        far = dot_tn(rows_of(i, 1), weight.astype(bf16))
        far = jnp.where(second, far[DH:], far[:DH])
        share = 1.0 / total
        outs.append(o_ref[h * DH : (h + 1) * DH] * (scale * share) + far * share)
    for pair in range(GROUP // 2):
        both = jnp.concatenate(outs[2 * pair : 2 * pair + 2], axis=0)
        at = (len(rest) - 1) * GROUP * DH + pair * LANES
        out_ref[:, at : at + LANES] = jnp.transpose(both).astype(bf16)


def on_device(inputs, queries, keys_values, slot_weight, slot_gain, slot_bias, bounds):
    tokens, width = inputs.shape
    shards = lax.axis_size(SEQ)
    shard = lax.axis_index(SEQ)
    split = jnp.where(bounds[0, 0] > 0, bounds[0, 0], bounds[1, 0])
    base = shard * tokens
    yh, c = lax.axis_index("yh"), lax.axis_index("c")
    scal = jnp.stack(
        [
            split - base,
            base,
            jnp.int32(shards * tokens),
            yh * 2 + c,
            yh * 2 + 1 - c,
            (1 - yh) * 2 + c,
            (1 - yh) * 2 + 1 - c,
        ]
    ).astype(jnp.int32)
    x2 = lax.ppermute(inputs, "yh", SWAP)
    x1 = lax.ppermute(inputs, "c", SWAP)
    x3 = lax.ppermute(x2, "c", SWAP)
    up = [(i, i + 1) for i in range(shards - 1)]
    down = [(j, i) for i, j in up]
    before = lax.ppermute(keys_values[:, tokens - W :], SEQ, up)
    after = lax.ppermute(keys_values[:, :W], SEQ, down)

    weight_t = jnp.swapaxes(slot_weight.reshape(4, width, HEADS * R), 1, 2)
    kvh = call(
        prep_kernel,
        jax.ShapeDtypeStruct((HEADS, tokens, 2 * LANES), bf16),
        1, 8, 0, 2 << 20,
    )(scal, keys_values)

    slots = HEADS * R
    flops = 2 * tokens * slots * width
    acc_shape = jax.ShapeDtypeStruct((slots, tokens), f32)
    acc = call(partial_kernel, acc_shape, 3, 16, 2 * flops, 5 << 20)(
        scal, inputs, x1, weight_t
    )
    acc = call(more_kernel, acc_shape, 3, 16, flops, 6 << 20)(scal, x2, weight_t, acc)
    arrived = []
    for g in range(HEADS // GROUP):
        owners = lax.axis_size(GATHER[g])
        count = GROUP * R // owners
        sent = pl.pallas_call(
            functools.partial(project_kernel, g, count),
            out_shape=jax.ShapeDtypeStruct((owners, 2 * count, LANES), bf16),
            in_specs=[SMEM] + [VMEM] * 4,
            out_specs=pl.BlockSpec(memory_space=pltpu.HBM),
            scratch_shapes=[
                pltpu.VMEM((GROUP, R // count, 2 * count, LANES), bf16),
                pltpu.SemaphoreType.DMA((GROUP,)),
            ],
            compiler_params=pltpu.CompilerParams(vmem_limit_bytes=16 << 20),
            cost_estimate=pl.CostEstimate(
                flops=flops, bytes_accessed=3 << 20, transcendentals=tokens * slots // 2
            ),
        )(scal, x3, weight_t, acc, kvh)
        arrived.append(lax.all_to_all(sent, GATHER[g], 0, 0, tiled=True))

    near, stats, q2 = call(
        near_kernel,
        [
            jax.ShapeDtypeStruct((HEADS * DH, tokens), f32),
            jax.ShapeDtypeStruct((4 * HEADS, tokens), f32),
            jax.ShapeDtypeStruct((HEADS, tokens, LANES), bf16),
        ],
        4, 8, 4 * tokens * 3 * W * HEADS * LANES, 2 << 20, tokens * 3 * W * HEADS,
    )(scal, queries, keys_values, before, after)

    place = {name: lax.axis_size(name) for name in SEQ}
    stride = {"z": place["yl"] * place["x"], "yl": place["x"], "x": 1}
    outs = []
    tables = []
    for g in range(HEADS // GROUP):
        owners = lax.axis_size(GATHER[g])
        count = GROUP * R // owners
        first, inner = GATHER[g]
        starts = [
            ((k // place[inner]) * stride[first] + k % place[inner] * stride[inner]) * tokens
            for k in range(owners)
        ]
        line = lax.axis_index(SHARE[g]) * stride[SHARE[g]]
        edge = split // tokens
        in_line = (edge // stride[SHARE[g]]) % place[SHARE[g]] == lax.axis_index(SHARE[g])
        edge_slot = (edge // stride[first]) % place[first] * place[inner]
        edge_slot = edge_slot + (edge // stride[inner]) % place[inner]
        has_edge = (split % tokens != 0) & in_line
        marks = jnp.stack(
            [split - line * tokens, jnp.where(has_edge, edge_slot, 0), has_edge]
        ).astype(jnp.int32)
        peers = place[SHARE[g]]
        held = call(
            functools.partial(combine_kernel, starts, tokens, count),
            jax.ShapeDtypeStruct((peers, 2 * count, LANES), f32),
            1, 8, 0, 1 << 19, 1 << 16,
            scratch=[pltpu.VMEM((owners, count, LANES), f32)] * 2,
        )(marks, arrived[g])
        shared = lax.all_to_all(held, SHARE[g], 0, 0, tiled=True)
        head = g * GROUP + lax.div(lax.axis_index(GATHER[g]) * count, R)
        gain = lax.dynamic_slice_in_dim(slot_gain, head * DH, DH, 1).reshape(1, 2 * DH)
        bias = lax.dynamic_slice_in_dim(slot_bias, head * DH, DH, 1).reshape(1, 2 * DH)
        chunk = call(
            norm_kernel,
            jax.ShapeDtypeStruct((owners, 2 * count, LANES), bf16),
            3, 8, 0, 1 << 19, 1 << 14, 0,
        )(shared, gain, bias)
        tables.append(lax.all_to_all(chunk, GATHER[g], 0, 0, tiled=True))

    for g in range(HEADS // GROUP):
        outs.append(
            call(
                functools.partial(far_kernel, g),
                jax.ShapeDtypeStruct((tokens, (g + 1) * GROUP * DH), bf16),
                4 + g, 8, 2 * tokens * R * HEADS * LANES, 1 << 20, tokens * R * GROUP, 0,
            )(q2, tables[g], near, stats, *outs)
        )
    return outs[-1]


def solution(mesh):
    finer = Mesh(mesh.devices.reshape(8, 4, 4, 2, 2), SEQ + DOC)
    return jax.shard_map(
        on_device,
        mesh=finer,
        in_specs=(
            P(SEQ, DOC),
            P(SEQ, DOC),
            P(None, SEQ, DOC),
            P(None, DOC),
            P(None, DOC),
            P(None, DOC),
            P(None, SEQ),
        ),
        out_specs=P(SEQ, DOC),
        check_vma=False,
    )
```

```python
import functools

import jax
import jax.numpy as jnp
from jax import lax
from jax.experimental import pallas as pl
from jax.experimental.pallas import tpu as pltpu
from jax.sharding import Mesh
from jax.sharding import PartitionSpec as P


DH = 64
R = 256
W = 128
HEADS = 4
LANES = 128
GROUP = 4
COUNT = 8
SEQ = ("z", "yl", "x")
DOC = ("yh", "c")
EPS = 1e-05
LOW = -1e30
SWAP = [(0, 1), (1, 0)]

f32 = jnp.float32
bf16 = jnp.bfloat16
VMEM = pl.BlockSpec(memory_space=pltpu.VMEM)


def call(kernel, out_shape, n_in, vmem_mib, flops, nbytes, exps=0, scalars=1, scratch=()):
    single = not isinstance(out_shape, (list, tuple))
    return pl.pallas_call(
        kernel,
        out_shape=out_shape,
        in_specs=[VMEM] * (scalars + n_in),
        out_specs=VMEM if single else [VMEM] * len(out_shape),
        scratch_shapes=list(scratch),
        compiler_params=pltpu.CompilerParams(vmem_limit_bytes=vmem_mib << 20),
        cost_estimate=pl.CostEstimate(flops=flops, bytes_accessed=nbytes, transcendentals=exps),
    )


def dot_nt(a, b):
    return lax.dot_general(a, b, (((1,), (1,)), ((), ())), preferred_element_type=f32)


def dot_nn(a, b):
    return jnp.dot(a, b, preferred_element_type=f32)


def dot_tn(a, b):
    return lax.dot_general(a, b, (((0,), (0,)), ((), ())), preferred_element_type=f32)


def lanes_of(shape):
    return lax.broadcasted_iota(jnp.int32, shape, len(shape) - 1)


def prep_kernel(scal, kv_ref, kvh_ref):
    tokens = kv_ref.shape[1]
    local = scal[0, 0]
    second = lax.broadcasted_iota(jnp.int32, (tokens, LANES), 0) >= local
    left = lanes_of((tokens, LANES)) < DH
    for pair in range(HEADS // 2):
        cols = slice(pair * LANES, (pair + 1) * LANES)
        keys = kv_ref[0, :, cols].astype(f32)
        values = kv_ref[1, :, cols].astype(f32)
        keys_r = pltpu.roll(keys, DH, 1)
        values_r = pltpu.roll(values, DH, 1)
        for half in range(2):
            h = 2 * pair + half
            joined = jnp.where(left, keys, values_r) if half == 0 else jnp.where(left, keys_r, values)
            kvh_ref[h, :, :LANES] = jnp.where(second, 0.0, joined).astype(bf16)
            kvh_ref[h, :, LANES:] = jnp.where(second, joined, 0.0).astype(bf16)


def near_kernel(scal, q_ref, kv_ref, before_ref, after_ref, o_ref, stat_ref, q2_ref):
    tokens = q_ref.shape[0]
    local, base, total = scal[0, 0], scal[0, 1], scal[0, 2]
    blocks = tokens // W
    span = 3 * W
    key = lax.broadcasted_iota(jnp.int32, (span, W), 0)
    query_at = lax.broadcasted_iota(jnp.int32, (span, W), 1)
    band = (key >= query_at) & (key - query_at <= 2 * W)
    left = lanes_of((W, LANES)) < DH
    place = lax.broadcasted_iota(jnp.int32, (W, LANES), 0)
    stat_ref[...] = jnp.zeros_like(stat_ref)

    def piece(s, at, cols):
        if at < 0:
            return before_ref[s, :, cols]
        if at >= blocks:
            return after_ref[s, :, cols]
        return kv_ref[s, at * W : (at + 1) * W, cols]

    for b in range(blocks):
        here = slice(b * W, (b + 1) * W)
        query_pos = query_at + b * W
        key_pos = key + (b - 1) * W
        allowed = (
            band
            & ((query_pos >= local) == (key_pos >= local))
            & (key_pos + base >= 0)
            & (key_pos + base < total)
        )
        second = place + b * W >= local
        stat_ref[HEADS : HEADS + 1, here] = jnp.where(query_pos[:1] >= local, 1.0, 0.0)
        for pair in range(HEADS // 2):
            cols = slice(pair * LANES, (pair + 1) * LANES)
            query = q_ref[here, cols].astype(f32) * 0.125
            query_r = pltpu.roll(query, DH, 1)
            keys = jnp.concatenate([piece(0, b + i, cols) for i in (-1, 0, 1)], axis=0)
            values = jnp.concatenate([piece(1, b + i, cols) for i in (-1, 0, 1)], axis=0)
            for half in range(2):
                h = 2 * pair + half
                both = jnp.where(left, query, query_r) if half == 0 else jnp.where(left, query_r, query)
                q2_ref[h, here] = jnp.where(left == second, 0.0, both).astype(bf16)
                mine = jnp.where(left if half == 0 else jnp.logical_not(left), query, 0.0).astype(bf16)
                scores = jnp.where(allowed, dot_nt(keys, mine), LOW)
                top = jnp.max(scores, axis=0, keepdims=True)
                weight = jnp.exp(scores - top)
                stat_ref[h : h + 1, here] = top
                stat_ref[2 * HEADS + h : 2 * HEADS + h + 1, here] = jnp.sum(
                    weight, axis=0, keepdims=True
                )
                out = dot_tn(values, weight.astype(bf16))
                o_ref[h * DH : (h + 1) * DH, here] = out[half * DH : (half + 1) * DH]


def pieces_of(top):
    a = top.astype(bf16).astype(f32)
    b = (top - a).astype(bf16).astype(f32)
    return a, b, top - a - b


def partial_kernel(scal, x0, x1, wt_ref, acc_ref):
    acc_ref[...] = dot_nt(wt_ref[scal[0, 3]], x0[...]) + dot_nt(wt_ref[scal[0, 4]], x1[...])


def more_kernel(scal, x2, wt_ref, acc_ref, out_ref):
    out_ref[...] = acc_ref[...] + dot_nt(wt_ref[scal[0, 5]], x2[...])


def project_kernel(group, count, scal, x3, wt_ref, acc_ref, kvh_ref, out_ref, held, sems):
    tokens = x3.shape[0]
    local = scal[0, 0]
    mixed = jnp.logical_and(local > 0, local < tokens)
    lane = lanes_of((R, LANES))
    at_a = lane == 0
    at_b = lane == DH
    left = lane < DH
    parts = R // count

    def logits_of(i):
        at = (group * GROUP + i) * R
        rows = slice(at, at + R)
        return acc_ref[rows, :] + dot_nt(wt_ref[scal[0, 6], rows, :], x3[...])

    def from_first(n):
        return n - jnp.where(left, n[:, 0:1], n[:, DH : DH + 1])

    def put(i, hi, rest):
        packed = jnp.concatenate(
            [hi.reshape(parts, count, LANES), rest.reshape(parts, count, LANES)], axis=1
        )
        held[i] = packed.astype(bf16)
        copy = pltpu.make_async_copy(
            held.at[i], out_ref.at[pl.ds(i * parts, parts)], sems.at[i]
        )
        copy.start()
        return copy

    @pl.when(jnp.logical_not(mixed))
    def _():
        side = pl.multiple_of(jnp.where(local <= 0, LANES, 0), LANES)
        copies = []
        after = logits_of(0)
        for i in range(GROUP):
            h = group * GROUP + i
            logits = after
            if i + 1 < GROUP:
                after = logits_of(i + 1)
            a, b, c = pieces_of(jnp.max(logits, axis=1, keepdims=True))
            proj = jnp.exp(logits - (a + b)).astype(bf16)
            n = from_first(dot_nn(proj, kvh_ref[h, :, pl.ds(side, LANES)]))
            hi = n.astype(bf16).astype(f32)
            rest = jnp.where(at_a, c, jnp.where(at_b, 0.0, n - hi))
            hi = jnp.where(at_a, a, jnp.where(at_b, b, hi))
            copies.append(put(i, hi, rest))
        for copy in copies:
            copy.wait()

    @pl.when(mixed)
    def _():
        second = lax.broadcasted_iota(jnp.int32, (R, tokens), 1) >= local
        copies = []
        for i in range(GROUP):
            h = group * GROUP + i
            logits = logits_of(i)
            a0, b0, _ = pieces_of(jnp.max(jnp.where(second, LOW, logits), axis=1, keepdims=True))
            a1, b1, _ = pieces_of(jnp.max(jnp.where(second, logits, LOW), axis=1, keepdims=True))
            proj = jnp.exp(logits - jnp.where(second, a1 + b1, a0 + b0)).astype(bf16)
            sums = dot_nn(proj, kvh_ref[h])
            n0 = from_first(sums[:, :LANES])
            n1 = from_first(sums[:, LANES:])
            n0 = jnp.where(at_a, a0, jnp.where(at_b, b0, n0))
            n1 = jnp.where(at_a, a1, jnp.where(at_b, b1, n1))
            copies.append(put(i, n0, n1))
        for copy in copies:
            copy.wait()


def combine_kernel(tokens, scal, in_ref, gain_ref, bias_ref, out_ref, marks):
    senders = in_ref.shape[0]
    slot = scal[0, 1]
    has_edge = scal[0, 2] > 0
    shape = (COUNT, LANES)
    row = lax.broadcasted_iota(jnp.int32, (LANES, 2 * LANES), 0)
    col = lanes_of((LANES, 2 * LANES))
    pick = jnp.where((row == 0) | ((row == DH) & (col < LANES)), 1.0, 0.0).astype(bf16)
    marks[...] = dot_nn(in_ref[...].reshape(senders * 2 * COUNT, LANES), pick).reshape(marks.shape)
    low = jnp.full(shape, LOW, f32)
    border = jnp.full(shape, scal[0, 0], jnp.int32)
    extra = in_ref[slot].astype(f32)[COUNT:]
    extra_top = jnp.where(has_edge, marks[slot][COUNT:, :LANES], low)
    top0, full0, top1, full1 = low, low, extra_top, extra_top
    for k in range(senders):
        late = border <= k * tokens
        is_edge = jnp.logical_and(border > k * tokens, border < (k + 1) * tokens)
        top = marks[k, :COUNT, :LANES]
        full = top + jnp.where(is_edge, 0.0, marks[k, COUNT:, LANES:])
        top0 = jnp.maximum(top0, jnp.where(late, low, top))
        full0 = jnp.maximum(full0, jnp.where(late, low, full))
        top1 = jnp.maximum(top1, jnp.where(late, top, low))
        full1 = jnp.maximum(full1, jnp.where(late, full, low))
    n0 = jnp.zeros(shape, f32)
    n1 = jnp.where(has_edge, extra * jnp.exp(extra_top - top1), 0.0)
    for k in range(senders):
        late = border <= k * tokens
        is_edge = jnp.logical_and(border > k * tokens, border < (k + 1) * tokens)
        got = in_ref[k].astype(f32)
        value = got[:COUNT] + jnp.where(is_edge, 0.0, got[COUNT:])
        value = value * jnp.exp(marks[k, :COUNT, :LANES] - jnp.where(late, top1, top0))
        n0 = n0 + jnp.where(late, 0.0, value)
        n1 = n1 + jnp.where(late, value, 0.0)
    lane = lanes_of(shape)
    left = lane < DH
    used = jnp.logical_and(lane != 0, lane != DH)

    def halves(v):
        a = jnp.sum(jnp.where(left, v, 0.0), axis=1, keepdims=True)
        b = jnp.sum(jnp.where(left, 0.0, v), axis=1, keepdims=True)
        return jnp.where(left, a, b) * (1.0 / DH)

    def norm(n, top, full):
        n = jnp.where(used, n, 0.0)
        centred = n - halves(n)
        variance = halves(centred * centred)
        scale = jnp.exp(2.0 * (full - top))
        return centred * lax.rsqrt(variance + EPS * scale) * gain_ref[...] + bias_ref[...]

    t0 = norm(n0, top0, full0)
    t1 = norm(n1, top1, full1)
    keys = jnp.where(left, t0, pltpu.roll(t1, DH, 1))
    values = jnp.where(left, pltpu.roll(t0, DH, 1), t1)
    chunk = jnp.concatenate([keys, values], axis=0).astype(bf16)[None]
    out_ref[...] = jnp.broadcast_to(chunk, out_ref.shape)


def far_kernel(group, q2_ref, tab_ref, o_ref, stat_ref, *rest):
    out_ref = rest[-1]
    count = tab_ref.shape[1] // 2
    parts = R // count
    second = stat_ref[HEADS : HEADS + 1, :] > 0.5
    for i, done in enumerate(rest[:-1]):
        out_ref[:, i * LANES : (i + 1) * LANES] = done[...]

    def rows_of(i, part):
        got = tab_ref[i * parts : (i + 1) * parts].astype(f32)
        return got[:, part * count : (part + 1) * count].reshape(R, LANES).astype(bf16)

    def scores_of(i):
        return dot_nt(rows_of(i, 0), q2_ref[group * GROUP + i])

    after = scores_of(0)
    outs = []
    for i in range(GROUP):
        h = group * GROUP + i
        scores = after
        if i + 1 < GROUP:
            after = scores_of(i + 1)
        near_top = stat_ref[h : h + 1, :]
        near_total = stat_ref[2 * HEADS + h : 2 * HEADS + h + 1, :]
        top = jnp.maximum(jnp.max(scores, axis=0, keepdims=True), near_top)
        weight = jnp.exp(scores - top)
        scale = jnp.exp(near_top - top)
        total = jnp.sum(weight, axis=0, keepdims=True) + near_total * scale
        far = dot_tn(rows_of(i, 1), weight.astype(bf16))
        far = jnp.where(second, far[DH:], far[:DH])
        share = 1.0 / total
        outs.append(o_ref[h * DH : (h + 1) * DH] * (scale * share) + far * share)
    for pair in range(GROUP // 2):
        both = jnp.concatenate(outs[2 * pair : 2 * pair + 2], axis=0)
        at = (len(rest) - 1) * GROUP * DH + pair * LANES
        out_ref[:, at : at + LANES] = jnp.transpose(both).astype(bf16)


def on_device(inputs, queries, keys_values, slot_weight, slot_gain, slot_bias, bounds):
    tokens, width = inputs.shape
    shards = lax.axis_size(SEQ)
    shard = lax.axis_index(SEQ)
    split = jnp.where(bounds[0, 0] > 0, bounds[0, 0], bounds[1, 0])
    base = shard * tokens
    yh, c = lax.axis_index("yh"), lax.axis_index("c")
    scal = jnp.stack(
        [
            split - base,
            base,
            jnp.int32(shards * tokens),
            yh * 2 + c,
            yh * 2 + 1 - c,
            (1 - yh) * 2 + c,
            (1 - yh) * 2 + 1 - c,
        ]
    ).astype(jnp.int32)[None]
    x2 = lax.ppermute(inputs, "yh", SWAP)
    x1 = lax.ppermute(inputs, "c", SWAP)
    x3 = lax.ppermute(x2, "c", SWAP)
    up = [(i, i + 1) for i in range(shards - 1)]
    down = [(j, i) for i, j in up]
    before = lax.ppermute(keys_values[:, tokens - W :], SEQ, up)
    after = lax.ppermute(keys_values[:, :W], SEQ, down)

    weight_t = jnp.swapaxes(slot_weight.reshape(4, width, HEADS * R), 1, 2)
    kvh = call(
        prep_kernel,
        jax.ShapeDtypeStruct((HEADS, tokens, 2 * LANES), bf16),
        1, 8, 0, 2 << 20,
    )(scal, keys_values)

    slots = HEADS * R
    flops = 2 * tokens * slots * width
    acc_shape = jax.ShapeDtypeStruct((slots, tokens), f32)
    acc = call(partial_kernel, acc_shape, 3, 16, 2 * flops, 5 << 20)(
        scal, inputs, x1, weight_t
    )
    acc = call(more_kernel, acc_shape, 3, 16, flops, 6 << 20)(scal, x2, weight_t, acc)
    arrived = []
    for g in range(HEADS // GROUP):
        owners = shards
        count = COUNT
        sent = pl.pallas_call(
            functools.partial(project_kernel, g, count),
            out_shape=jax.ShapeDtypeStruct((owners, 2 * count, LANES), bf16),
            in_specs=[VMEM] * 5,
            out_specs=pl.BlockSpec(memory_space=pltpu.HBM),
            scratch_shapes=[
                pltpu.VMEM((GROUP, R // count, 2 * count, LANES), bf16),
                pltpu.SemaphoreType.DMA((GROUP,)),
            ],
            compiler_params=pltpu.CompilerParams(vmem_limit_bytes=16 << 20),
            cost_estimate=pl.CostEstimate(
                flops=flops, bytes_accessed=3 << 20, transcendentals=tokens * slots // 2
            ),
        )(scal, x3, weight_t, acc, kvh)
        arrived.append(lax.all_to_all(sent, SEQ, 0, 0, tiled=True))

    near, stats, q2 = call(
        near_kernel,
        [
            jax.ShapeDtypeStruct((HEADS * DH, tokens), f32),
            jax.ShapeDtypeStruct((4 * HEADS, tokens), f32),
            jax.ShapeDtypeStruct((HEADS, tokens, LANES), bf16),
        ],
        4, 8, 4 * tokens * 3 * W * HEADS * LANES, 2 << 20, tokens * 3 * W * HEADS,
    )(scal, queries, keys_values, before, after)

    outs = []
    edge = split // tokens
    has_edge = split % tokens != 0
    marks = jnp.stack([split, jnp.where(has_edge, edge, 0), has_edge]).astype(jnp.int32)[None]
    head = lax.div(shard * COUNT, R)
    gain = lax.dynamic_slice_in_dim(slot_gain, head * DH, DH, 1).reshape(1, 2 * DH)
    bias = lax.dynamic_slice_in_dim(slot_bias, head * DH, DH, 1).reshape(1, 2 * DH)
    chunk = call(
        functools.partial(combine_kernel, tokens),
        jax.ShapeDtypeStruct((shards, 2 * COUNT, LANES), bf16),
        3, 10, 0, 1 << 20, 1 << 17,
        scratch=[pltpu.VMEM((shards, 2 * COUNT, 2 * LANES), f32)],
    )(marks, arrived[0], gain, bias)
    tables = [lax.all_to_all(chunk, SEQ, 0, 0, tiled=True)]

    for g in range(HEADS // GROUP):
        outs.append(
            call(
                functools.partial(far_kernel, g),
                jax.ShapeDtypeStruct((tokens, (g + 1) * GROUP * DH), bf16),
                4 + g, 8, 2 * tokens * R * HEADS * LANES, 1 << 20, tokens * R * GROUP, 0,
            )(q2, tables[g], near, stats, *outs)
        )
    return outs[-1]


def solution(mesh):
    finer = Mesh(mesh.devices.reshape(8, 4, 4, 2, 2), SEQ + DOC)
    return jax.shard_map(
        on_device,
        mesh=finer,
        in_specs=(
            P(SEQ, DOC),
            P(SEQ, DOC),
            P(None, SEQ, DOC),
            P(None, DOC),
            P(None, DOC),
            P(None, DOC),
            P(None, SEQ),
        ),
        out_specs=P(SEQ, DOC),
        check_vma=False,
    )
```

```python
import functools

import jax
import jax.numpy as jnp
from jax import lax
from jax.experimental import pallas as pl
from jax.experimental.pallas import tpu as pltpu
from jax.sharding import Mesh
from jax.sharding import PartitionSpec as P


DH = 64
R = 256
W = 128
HEADS = 4
LANES = 128
GROUP = 4
COUNT = 8
ORDER = ("yl", "x", "z")
SEQ = ("z", "yl", "x")
DOC = ("yh", "c")
EPS = 1e-05
LOW = -1e30
SWAP = [(0, 1), (1, 0)]

f32 = jnp.float32
bf16 = jnp.bfloat16
VMEM = pl.BlockSpec(memory_space=pltpu.VMEM)


def call(kernel, out_shape, n_in, vmem_mib, flops, nbytes, exps=0, scalars=1, scratch=()):
    single = not isinstance(out_shape, (list, tuple))
    return pl.pallas_call(
        kernel,
        out_shape=out_shape,
        in_specs=[VMEM] * (scalars + n_in),
        out_specs=VMEM if single else [VMEM] * len(out_shape),
        scratch_shapes=list(scratch),
        compiler_params=pltpu.CompilerParams(vmem_limit_bytes=vmem_mib << 20),
        cost_estimate=pl.CostEstimate(flops=flops, bytes_accessed=nbytes, transcendentals=exps),
    )


def dot_nt(a, b):
    return lax.dot_general(a, b, (((1,), (1,)), ((), ())), preferred_element_type=f32)


def dot_nn(a, b):
    return jnp.dot(a, b, preferred_element_type=f32)


def dot_tn(a, b):
    return lax.dot_general(a, b, (((0,), (0,)), ((), ())), preferred_element_type=f32)


def lanes_of(shape):
    return lax.broadcasted_iota(jnp.int32, shape, len(shape) - 1)


def prep_kernel(scal, kv_ref, kvh_ref):
    tokens = kv_ref.shape[1]
    local = scal[0, 0]
    second = lax.broadcasted_iota(jnp.int32, (tokens, LANES), 0) >= local
    left = lanes_of((tokens, LANES)) < DH
    for pair in range(HEADS // 2):
        cols = slice(pair * LANES, (pair + 1) * LANES)
        keys = kv_ref[0, :, cols].astype(f32)
        values = kv_ref[1, :, cols].astype(f32)
        keys_r = pltpu.roll(keys, DH, 1)
        values_r = pltpu.roll(values, DH, 1)
        for half in range(2):
            h = 2 * pair + half
            joined = jnp.where(left, keys, values_r) if half == 0 else jnp.where(left, keys_r, values)
            kvh_ref[h, :, :LANES] = jnp.where(second, 0.0, joined).astype(bf16)
            kvh_ref[h, :, LANES:] = jnp.where(second, joined, 0.0).astype(bf16)


def near_kernel(scal, q_ref, kv_ref, before_ref, after_ref, o_ref, stat_ref, q2_ref):
    tokens = q_ref.shape[0]
    local, base, total = scal[0, 0], scal[0, 1], scal[0, 2]
    blocks = tokens // W
    span = 3 * W
    key = lax.broadcasted_iota(jnp.int32, (span, W), 0)
    query_at = lax.broadcasted_iota(jnp.int32, (span, W), 1)
    band = (key >= query_at) & (key - query_at <= 2 * W)
    left = lanes_of((W, LANES)) < DH
    place = lax.broadcasted_iota(jnp.int32, (W, LANES), 0)
    stat_ref[...] = jnp.zeros_like(stat_ref)

    def piece(s, at, cols):
        if at < 0:
            return before_ref[s, :, cols]
        if at >= blocks:
            return after_ref[s, :, cols]
        return kv_ref[s, at * W : (at + 1) * W, cols]

    for b in range(blocks):
        here = slice(b * W, (b + 1) * W)
        query_pos = query_at + b * W
        key_pos = key + (b - 1) * W
        allowed = (
            band
            & ((query_pos >= local) == (key_pos >= local))
            & (key_pos + base >= 0)
            & (key_pos + base < total)
        )
        second = place + b * W >= local
        stat_ref[HEADS : HEADS + 1, here] = jnp.where(query_pos[:1] >= local, 1.0, 0.0)
        for pair in range(HEADS // 2):
            cols = slice(pair * LANES, (pair + 1) * LANES)
            query = q_ref[here, cols].astype(f32) * 0.125
            query_r = pltpu.roll(query, DH, 1)
            keys = jnp.concatenate([piece(0, b + i, cols) for i in (-1, 0, 1)], axis=0)
            values = jnp.concatenate([piece(1, b + i, cols) for i in (-1, 0, 1)], axis=0)
            for half in range(2):
                h = 2 * pair + half
                both = jnp.where(left, query, query_r) if half == 0 else jnp.where(left, query_r, query)
                q2_ref[h, here] = jnp.where(left == second, 0.0, both).astype(bf16)
                mine = jnp.where(left if half == 0 else jnp.logical_not(left), query, 0.0).astype(bf16)
                scores = jnp.where(allowed, dot_nt(keys, mine), LOW)
                top = jnp.max(scores, axis=0, keepdims=True)
                weight = jnp.exp(scores - top)
                stat_ref[h : h + 1, here] = top
                stat_ref[2 * HEADS + h : 2 * HEADS + h + 1, here] = jnp.sum(
                    weight, axis=0, keepdims=True
                )
                out = dot_tn(values, weight.astype(bf16))
                o_ref[h * DH : (h + 1) * DH, here] = out[half * DH : (half + 1) * DH]


def pieces_of(top):
    a = top.astype(bf16).astype(f32)
    b = (top - a).astype(bf16).astype(f32)
    return a, b, top - a - b


def partial_kernel(scal, x0, x1, wt_ref, acc_ref):
    acc_ref[...] = dot_nt(wt_ref[scal[0, 3]], x0[...]) + dot_nt(wt_ref[scal[0, 4]], x1[...])


def more_kernel(scal, x2, wt_ref, acc_ref, out_ref):
    out_ref[...] = acc_ref[...] + dot_nt(wt_ref[scal[0, 5]], x2[...])


def project_kernel(group, count, scal, x3, wt_ref, acc_ref, kvh_ref, out_ref, held, sems):
    tokens = x3.shape[0]
    local = scal[0, 0]
    mixed = jnp.logical_and(local > 0, local < tokens)
    lane = lanes_of((R, LANES))
    at_a = lane == 0
    at_b = lane == DH
    left = lane < DH
    parts = R // count

    def logits_of(i):
        at = (group * GROUP + i) * R
        rows = slice(at, at + R)
        return acc_ref[rows, :] + dot_nt(wt_ref[scal[0, 6], rows, :], x3[...])

    def from_first(n):
        return n - jnp.where(left, n[:, 0:1], n[:, DH : DH + 1])

    def put(i, hi, rest):
        packed = jnp.concatenate(
            [hi.reshape(parts, count, LANES), rest.reshape(parts, count, LANES)], axis=1
        )
        held[i] = packed.astype(bf16)
        copy = pltpu.make_async_copy(
            held.at[i], out_ref.at[pl.ds(i * parts, parts)], sems.at[i]
        )
        copy.start()
        return copy

    @pl.when(jnp.logical_not(mixed))
    def _():
        side = pl.multiple_of(jnp.where(local <= 0, LANES, 0), LANES)
        copies = []
        after = logits_of(0)
        for i in range(GROUP):
            h = group * GROUP + i
            logits = after
            if i + 1 < GROUP:
                after = logits_of(i + 1)
            a, b, c = pieces_of(jnp.max(logits, axis=1, keepdims=True))
            proj = jnp.exp(logits - (a + b)).astype(bf16)
            n = from_first(dot_nn(proj, kvh_ref[h, :, pl.ds(side, LANES)]))
            hi = n.astype(bf16).astype(f32)
            rest = jnp.where(at_a, c, jnp.where(at_b, 0.0, n - hi))
            hi = jnp.where(at_a, a, jnp.where(at_b, b, hi))
            copies.append(put(i, hi, rest))
        for copy in copies:
            copy.wait()

    @pl.when(mixed)
    def _():
        second = lax.broadcasted_iota(jnp.int32, (R, tokens), 1) >= local
        copies = []
        for i in range(GROUP):
            h = group * GROUP + i
            logits = logits_of(i)
            a0, b0, _ = pieces_of(jnp.max(jnp.where(second, LOW, logits), axis=1, keepdims=True))
            a1, b1, _ = pieces_of(jnp.max(jnp.where(second, logits, LOW), axis=1, keepdims=True))
            proj = jnp.exp(logits - jnp.where(second, a1 + b1, a0 + b0)).astype(bf16)
            sums = dot_nn(proj, kvh_ref[h])
            n0 = from_first(sums[:, :LANES])
            n1 = from_first(sums[:, LANES:])
            n0 = jnp.where(at_a, a0, jnp.where(at_b, b0, n0))
            n1 = jnp.where(at_a, a1, jnp.where(at_b, b1, n1))
            copies.append(put(i, n0, n1))
        for copy in copies:
            copy.wait()


def combine_kernel(starts, tokens, scal, in_ref, gain_ref, bias_ref, out_ref, marks):
    senders = in_ref.shape[0]
    slot = scal[0, 1]
    has_edge = scal[0, 2] > 0
    shape = (COUNT, LANES)
    row = lax.broadcasted_iota(jnp.int32, (LANES, 2 * LANES), 0)
    col = lanes_of((LANES, 2 * LANES))
    pick = jnp.where((row == 0) | ((row == DH) & (col < LANES)), 1.0, 0.0).astype(bf16)
    marks[...] = dot_nn(in_ref[...].reshape(senders * 2 * COUNT, LANES), pick).reshape(marks.shape)
    low = jnp.full(shape, LOW, f32)
    border = jnp.full(shape, scal[0, 0], jnp.int32)
    extra = in_ref[slot].astype(f32)[COUNT:]
    extra_top = jnp.where(has_edge, marks[slot][COUNT:, :LANES], low)
    top0, full0, top1, full1 = low, low, extra_top, extra_top
    for k in range(senders):
        late = border <= starts[k]
        is_edge = jnp.logical_and(border > starts[k], border < starts[k] + tokens)
        top = marks[k, :COUNT, :LANES]
        full = top + jnp.where(is_edge, 0.0, marks[k, COUNT:, LANES:])
        top0 = jnp.maximum(top0, jnp.where(late, low, top))
        full0 = jnp.maximum(full0, jnp.where(late, low, full))
        top1 = jnp.maximum(top1, jnp.where(late, top, low))
        full1 = jnp.maximum(full1, jnp.where(late, full, low))
    n0 = jnp.zeros(shape, f32)
    n1 = jnp.where(has_edge, extra * jnp.exp(extra_top - top1), 0.0)
    for k in range(senders):
        late = border <= starts[k]
        is_edge = jnp.logical_and(border > starts[k], border < starts[k] + tokens)
        got = in_ref[k].astype(f32)
        value = got[:COUNT] + jnp.where(is_edge, 0.0, got[COUNT:])
        value = value * jnp.exp(marks[k, :COUNT, :LANES] - jnp.where(late, top1, top0))
        n0 = n0 + jnp.where(late, 0.0, value)
        n1 = n1 + jnp.where(late, value, 0.0)
    lane = lanes_of(shape)
    left = lane < DH
    used = jnp.logical_and(lane != 0, lane != DH)

    def halves(v):
        a = jnp.sum(jnp.where(left, v, 0.0), axis=1, keepdims=True)
        b = jnp.sum(jnp.where(left, 0.0, v), axis=1, keepdims=True)
        return jnp.where(left, a, b) * (1.0 / DH)

    def norm(n, top, full):
        n = jnp.where(used, n, 0.0)
        centred = n - halves(n)
        variance = halves(centred * centred)
        scale = jnp.exp(2.0 * (full - top))
        return centred * lax.rsqrt(variance + EPS * scale) * gain_ref[...] + bias_ref[...]

    t0 = norm(n0, top0, full0)
    t1 = norm(n1, top1, full1)
    keys = jnp.where(left, t0, pltpu.roll(t1, DH, 1))
    values = jnp.where(left, pltpu.roll(t0, DH, 1), t1)
    chunk = jnp.concatenate([keys, values], axis=0).astype(bf16)[None]
    out_ref[...] = jnp.broadcast_to(chunk, out_ref.shape)


def far_kernel(group, q2_ref, tab_ref, o_ref, stat_ref, *rest):
    out_ref = rest[-1]
    count = tab_ref.shape[1] // 2
    parts = R // count
    second = stat_ref[HEADS : HEADS + 1, :] > 0.5
    for i, done in enumerate(rest[:-1]):
        out_ref[:, i * LANES : (i + 1) * LANES] = done[...]

    def rows_of(i, part):
        got = tab_ref[i * parts : (i + 1) * parts].astype(f32)
        return got[:, part * count : (part + 1) * count].reshape(R, LANES).astype(bf16)

    def scores_of(i):
        return dot_nt(rows_of(i, 0), q2_ref[group * GROUP + i])

    after = scores_of(0)
    outs = []
    for i in range(GROUP):
        h = group * GROUP + i
        scores = after
        if i + 1 < GROUP:
            after = scores_of(i + 1)
        near_top = stat_ref[h : h + 1, :]
        near_total = stat_ref[2 * HEADS + h : 2 * HEADS + h + 1, :]
        top = jnp.maximum(jnp.max(scores, axis=0, keepdims=True), near_top)
        weight = jnp.exp(scores - top)
        scale = jnp.exp(near_top - top)
        total = jnp.sum(weight, axis=0, keepdims=True) + near_total * scale
        far = dot_tn(rows_of(i, 1), weight.astype(bf16))
        far = jnp.where(second, far[DH:], far[:DH])
        share = 1.0 / total
        outs.append(o_ref[h * DH : (h + 1) * DH] * (scale * share) + far * share)
    for pair in range(GROUP // 2):
        both = jnp.concatenate(outs[2 * pair : 2 * pair + 2], axis=0)
        at = (len(rest) - 1) * GROUP * DH + pair * LANES
        out_ref[:, at : at + LANES] = jnp.transpose(both).astype(bf16)


def on_device(inputs, queries, keys_values, slot_weight, slot_gain, slot_bias, bounds):
    tokens, width = inputs.shape
    shards = lax.axis_size(SEQ)
    shard = lax.axis_index(SEQ)
    split = jnp.where(bounds[0, 0] > 0, bounds[0, 0], bounds[1, 0])
    base = shard * tokens
    yh, c = lax.axis_index("yh"), lax.axis_index("c")
    scal = jnp.stack(
        [
            split - base,
            base,
            jnp.int32(shards * tokens),
            yh * 2 + c,
            yh * 2 + 1 - c,
            (1 - yh) * 2 + c,
            (1 - yh) * 2 + 1 - c,
        ]
    ).astype(jnp.int32)[None]
    x2 = lax.ppermute(inputs, "yh", SWAP)
    x1 = lax.ppermute(inputs, "c", SWAP)
    x3 = lax.ppermute(x2, "c", SWAP)
    up = [(i, i + 1) for i in range(shards - 1)]
    down = [(j, i) for i, j in up]
    before = lax.ppermute(keys_values[:, tokens - W :], SEQ, up)
    after = lax.ppermute(keys_values[:, :W], SEQ, down)

    weight_t = jnp.swapaxes(slot_weight.reshape(4, width, HEADS * R), 1, 2)
    kvh = call(
        prep_kernel,
        jax.ShapeDtypeStruct((HEADS, tokens, 2 * LANES), bf16),
        1, 8, 0, 2 << 20,
    )(scal, keys_values)

    slots = HEADS * R
    flops = 2 * tokens * slots * width
    acc_shape = jax.ShapeDtypeStruct((slots, tokens), f32)
    acc = call(partial_kernel, acc_shape, 3, 16, 2 * flops, 5 << 20)(
        scal, inputs, x1, weight_t
    )
    acc = call(more_kernel, acc_shape, 3, 16, flops, 6 << 20)(scal, x2, weight_t, acc)
    arrived = []
    for g in range(HEADS // GROUP):
        owners = shards
        count = COUNT
        sent = pl.pallas_call(
            functools.partial(project_kernel, g, count),
            out_shape=jax.ShapeDtypeStruct((owners, 2 * count, LANES), bf16),
            in_specs=[VMEM] * 5,
            out_specs=pl.BlockSpec(memory_space=pltpu.HBM),
            scratch_shapes=[
                pltpu.VMEM((GROUP, R // count, 2 * count, LANES), bf16),
                pltpu.SemaphoreType.DMA((GROUP,)),
            ],
            compiler_params=pltpu.CompilerParams(vmem_limit_bytes=16 << 20),
            cost_estimate=pl.CostEstimate(
                flops=flops, bytes_accessed=3 << 20, transcendentals=tokens * slots // 2
            ),
        )(scal, x3, weight_t, acc, kvh)
        arrived.append(lax.all_to_all(sent, ORDER, 0, 0, tiled=True))

    near, stats, q2 = call(
        near_kernel,
        [
            jax.ShapeDtypeStruct((HEADS * DH, tokens), f32),
            jax.ShapeDtypeStruct((4 * HEADS, tokens), f32),
            jax.ShapeDtypeStruct((HEADS, tokens, LANES), bf16),
        ],
        4, 8, 4 * tokens * 3 * W * HEADS * LANES, 2 << 20, tokens * 3 * W * HEADS,
    )(scal, queries, keys_values, before, after)

    outs = []
    size = {name: lax.axis_size(name) for name in SEQ}
    stride = {"z": size["yl"] * size["x"], "yl": size["x"], "x": 1}
    a, b, c = ORDER
    starts = [
        tokens
        * (
            k // (size[b] * size[c]) * stride[a]
            + k // size[c] % size[b] * stride[b]
            + k % size[c] * stride[c]
        )
        for k in range(shards)
    ]
    at = split // tokens
    at = [at // stride[name] % size[name] for name in ORDER]
    edge = (at[0] * size[b] + at[1]) * size[c] + at[2]
    has_edge = split % tokens != 0
    marks = jnp.stack([split, jnp.where(has_edge, edge, 0), has_edge]).astype(jnp.int32)[None]
    head = lax.div(lax.axis_index(ORDER) * COUNT, R)
    gain = lax.dynamic_slice_in_dim(slot_gain, head * DH, DH, 1).reshape(1, 2 * DH)
    bias = lax.dynamic_slice_in_dim(slot_bias, head * DH, DH, 1).reshape(1, 2 * DH)
    chunk = call(
        functools.partial(combine_kernel, starts, tokens),
        jax.ShapeDtypeStruct((shards, 2 * COUNT, LANES), bf16),
        3, 10, 0, 1 << 20, 1 << 17,
        scratch=[pltpu.VMEM((shards, 2 * COUNT, 2 * LANES), f32)],
    )(marks, arrived[0], gain, bias)
    tables = [lax.all_to_all(chunk, ORDER, 0, 0, tiled=True)]

    for g in range(HEADS // GROUP):
        outs.append(
            call(
                functools.partial(far_kernel, g),
                jax.ShapeDtypeStruct((tokens, (g + 1) * GROUP * DH), bf16),
                4 + g, 8, 2 * tokens * R * HEADS * LANES, 1 << 20, tokens * R * GROUP, 0,
            )(q2, tables[g], near, stats, *outs)
        )
    return outs[-1]


def solution(mesh):
    finer = Mesh(mesh.devices.reshape(8, 4, 4, 2, 2), SEQ + DOC)
    return jax.shard_map(
        on_device,
        mesh=finer,
        in_specs=(
            P(SEQ, DOC),
            P(SEQ, DOC),
            P(None, SEQ, DOC),
            P(None, DOC),
            P(None, DOC),
            P(None, DOC),
            P(None, SEQ),
        ),
        out_specs=P(SEQ, DOC),
        check_vma=False,
    )
```

```python
import functools

import jax
import jax.numpy as jnp
from jax import lax
from jax.experimental import pallas as pl
from jax.experimental.pallas import tpu as pltpu
from jax.sharding import Mesh
from jax.sharding import PartitionSpec as P


DH = 64
R = 256
W = 128
HEADS = 4
LANES = 128
GROUP = 4
COUNT = 8
ORDER = ("yl", "x", "zl", "zh")
SEQ = ("zh", "zl", "yl", "x")
DOC = ("yh", "c")
EPS = 1e-05
LOW = -1e30
SWAP = [(0, 1), (1, 0)]

f32 = jnp.float32
bf16 = jnp.bfloat16
VMEM = pl.BlockSpec(memory_space=pltpu.VMEM)


def call(kernel, out_shape, n_in, vmem_mib, flops, nbytes, exps=0, scalars=1, scratch=()):
    single = not isinstance(out_shape, (list, tuple))
    return pl.pallas_call(
        kernel,
        out_shape=out_shape,
        in_specs=[VMEM] * (scalars + n_in),
        out_specs=VMEM if single else [VMEM] * len(out_shape),
        scratch_shapes=list(scratch),
        compiler_params=pltpu.CompilerParams(vmem_limit_bytes=vmem_mib << 20),
        cost_estimate=pl.CostEstimate(flops=flops, bytes_accessed=nbytes, transcendentals=exps),
    )


def dot_nt(a, b):
    return lax.dot_general(a, b, (((1,), (1,)), ((), ())), preferred_element_type=f32)


def dot_nn(a, b):
    return jnp.dot(a, b, preferred_element_type=f32)


def dot_tn(a, b):
    return lax.dot_general(a, b, (((0,), (0,)), ((), ())), preferred_element_type=f32)


def lanes_of(shape):
    return lax.broadcasted_iota(jnp.int32, shape, len(shape) - 1)


def prep_kernel(scal, kv_ref, kvh_ref):
    tokens = kv_ref.shape[1]
    local = scal[0, 0]
    second = lax.broadcasted_iota(jnp.int32, (tokens, LANES), 0) >= local
    left = lanes_of((tokens, LANES)) < DH
    for pair in range(HEADS // 2):
        cols = slice(pair * LANES, (pair + 1) * LANES)
        keys = kv_ref[0, :, cols].astype(f32)
        values = kv_ref[1, :, cols].astype(f32)
        keys_r = pltpu.roll(keys, DH, 1)
        values_r = pltpu.roll(values, DH, 1)
        for half in range(2):
            h = 2 * pair + half
            joined = jnp.where(left, keys, values_r) if half == 0 else jnp.where(left, keys_r, values)
            kvh_ref[h, :, :LANES] = jnp.where(second, 0.0, joined).astype(bf16)
            kvh_ref[h, :, LANES:] = jnp.where(second, joined, 0.0).astype(bf16)


def near_kernel(scal, q_ref, kv_ref, before_ref, after_ref, o_ref, stat_ref, q2_ref):
    tokens = q_ref.shape[0]
    local, base, total = scal[0, 0], scal[0, 1], scal[0, 2]
    blocks = tokens // W
    span = 3 * W
    key = lax.broadcasted_iota(jnp.int32, (span, W), 0)
    query_at = lax.broadcasted_iota(jnp.int32, (span, W), 1)
    band = (key >= query_at) & (key - query_at <= 2 * W)
    left = lanes_of((W, LANES)) < DH
    place = lax.broadcasted_iota(jnp.int32, (W, LANES), 0)
    stat_ref[...] = jnp.zeros_like(stat_ref)

    def piece(s, at, cols):
        if at < 0:
            return before_ref[s, :, cols]
        if at >= blocks:
            return after_ref[s, :, cols]
        return kv_ref[s, at * W : (at + 1) * W, cols]

    for b in range(blocks):
        here = slice(b * W, (b + 1) * W)
        query_pos = query_at + b * W
        key_pos = key + (b - 1) * W
        allowed = (
            band
            & ((query_pos >= local) == (key_pos >= local))
            & (key_pos + base >= 0)
            & (key_pos + base < total)
        )
        second = place + b * W >= local
        stat_ref[HEADS : HEADS + 1, here] = jnp.where(query_pos[:1] >= local, 1.0, 0.0)
        for pair in range(HEADS // 2):
            cols = slice(pair * LANES, (pair + 1) * LANES)
            query = q_ref[here, cols].astype(f32) * 0.125
            query_r = pltpu.roll(query, DH, 1)
            keys = jnp.concatenate([piece(0, b + i, cols) for i in (-1, 0, 1)], axis=0)
            values = jnp.concatenate([piece(1, b + i, cols) for i in (-1, 0, 1)], axis=0)
            for half in range(2):
                h = 2 * pair + half
                both = jnp.where(left, query, query_r) if half == 0 else jnp.where(left, query_r, query)
                q2_ref[h, here] = jnp.where(left == second, 0.0, both).astype(bf16)
                mine = jnp.where(left if half == 0 else jnp.logical_not(left), query, 0.0).astype(bf16)
                scores = jnp.where(allowed, dot_nt(keys, mine), LOW)
                top = jnp.max(scores, axis=0, keepdims=True)
                weight = jnp.exp(scores - top)
                stat_ref[h : h + 1, here] = top
                stat_ref[2 * HEADS + h : 2 * HEADS + h + 1, here] = jnp.sum(
                    weight, axis=0, keepdims=True
                )
                out = dot_tn(values, weight.astype(bf16))
                o_ref[h * DH : (h + 1) * DH, here] = out[half * DH : (half + 1) * DH]


def pieces_of(top):
    a = top.astype(bf16).astype(f32)
    b = (top - a).astype(bf16).astype(f32)
    return a, b, top - a - b


def partial_kernel(scal, x0, x1, wt_ref, acc_ref):
    acc_ref[...] = dot_nt(wt_ref[scal[0, 3]], x0[...]) + dot_nt(wt_ref[scal[0, 4]], x1[...])


def more_kernel(scal, x2, wt_ref, acc_ref, out_ref):
    out_ref[...] = acc_ref[...] + dot_nt(wt_ref[scal[0, 5]], x2[...])


def project_kernel(group, count, scal, x3, wt_ref, acc_ref, kvh_ref, out_ref, held, sems):
    tokens = x3.shape[0]
    local = scal[0, 0]
    mixed = jnp.logical_and(local > 0, local < tokens)
    lane = lanes_of((R, LANES))
    at_a = lane == 0
    at_b = lane == DH
    left = lane < DH
    parts = R // count

    def logits_of(i):
        at = (group * GROUP + i) * R
        rows = slice(at, at + R)
        return acc_ref[rows, :] + dot_nt(wt_ref[scal[0, 6], rows, :], x3[...])

    def from_first(n):
        return n - jnp.where(left, n[:, 0:1], n[:, DH : DH + 1])

    def put(i, hi, rest):
        packed = jnp.concatenate(
            [hi.reshape(parts, count, LANES), rest.reshape(parts, count, LANES)], axis=1
        )
        held[i] = packed.astype(bf16)
        copy = pltpu.make_async_copy(
            held.at[i], out_ref.at[pl.ds(i * parts, parts)], sems.at[i]
        )
        copy.start()
        return copy

    @pl.when(jnp.logical_not(mixed))
    def _():
        side = pl.multiple_of(jnp.where(local <= 0, LANES, 0), LANES)
        copies = []
        after = logits_of(0)
        for i in range(GROUP):
            h = group * GROUP + i
            logits = after
            if i + 1 < GROUP:
                after = logits_of(i + 1)
            a, b, c = pieces_of(jnp.max(logits, axis=1, keepdims=True))
            proj = jnp.exp(logits - (a + b)).astype(bf16)
            n = from_first(dot_nn(proj, kvh_ref[h, :, pl.ds(side, LANES)]))
            hi = n.astype(bf16).astype(f32)
            rest = jnp.where(at_a, c, jnp.where(at_b, 0.0, n - hi))
            hi = jnp.where(at_a, a, jnp.where(at_b, b, hi))
            copies.append(put(i, hi, rest))
        for copy in copies:
            copy.wait()

    @pl.when(mixed)
    def _():
        second = lax.broadcasted_iota(jnp.int32, (R, tokens), 1) >= local
        copies = []
        for i in range(GROUP):
            h = group * GROUP + i
            logits = logits_of(i)
            a0, b0, _ = pieces_of(jnp.max(jnp.where(second, LOW, logits), axis=1, keepdims=True))
            a1, b1, _ = pieces_of(jnp.max(jnp.where(second, logits, LOW), axis=1, keepdims=True))
            proj = jnp.exp(logits - jnp.where(second, a1 + b1, a0 + b0)).astype(bf16)
            sums = dot_nn(proj, kvh_ref[h])
            n0 = from_first(sums[:, :LANES])
            n1 = from_first(sums[:, LANES:])
            n0 = jnp.where(at_a, a0, jnp.where(at_b, b0, n0))
            n1 = jnp.where(at_a, a1, jnp.where(at_b, b1, n1))
            copies.append(put(i, n0, n1))
        for copy in copies:
            copy.wait()


def combine_kernel(starts, tokens, scal, in_ref, gain_ref, bias_ref, out_ref, marks):
    senders = in_ref.shape[0]
    slot = scal[0, 1]
    has_edge = scal[0, 2] > 0
    shape = (COUNT, LANES)
    row = lax.broadcasted_iota(jnp.int32, (LANES, 2 * LANES), 0)
    col = lanes_of((LANES, 2 * LANES))
    pick = jnp.where((row == 0) | ((row == DH) & (col < LANES)), 1.0, 0.0).astype(bf16)
    marks[...] = dot_nn(in_ref[...].reshape(senders * 2 * COUNT, LANES), pick).reshape(marks.shape)
    low = jnp.full(shape, LOW, f32)
    border = jnp.full(shape, scal[0, 0], jnp.int32)
    extra = in_ref[slot].astype(f32)[COUNT:]
    extra_top = jnp.where(has_edge, marks[slot][COUNT:, :LANES], low)
    top0, full0, top1, full1 = low, low, extra_top, extra_top
    for k in range(senders):
        late = border <= starts[k]
        is_edge = jnp.logical_and(border > starts[k], border < starts[k] + tokens)
        top = marks[k, :COUNT, :LANES]
        full = top + jnp.where(is_edge, 0.0, marks[k, COUNT:, LANES:])
        top0 = jnp.maximum(top0, jnp.where(late, low, top))
        full0 = jnp.maximum(full0, jnp.where(late, low, full))
        top1 = jnp.maximum(top1, jnp.where(late, top, low))
        full1 = jnp.maximum(full1, jnp.where(late, full, low))
    n0 = jnp.zeros(shape, f32)
    n1 = jnp.where(has_edge, extra * jnp.exp(extra_top - top1), 0.0)
    for k in range(senders):
        late = border <= starts[k]
        is_edge = jnp.logical_and(border > starts[k], border < starts[k] + tokens)
        got = in_ref[k].astype(f32)
        value = got[:COUNT] + jnp.where(is_edge, 0.0, got[COUNT:])
        value = value * jnp.exp(marks[k, :COUNT, :LANES] - jnp.where(late, top1, top0))
        n0 = n0 + jnp.where(late, 0.0, value)
        n1 = n1 + jnp.where(late, value, 0.0)
    lane = lanes_of(shape)
    left = lane < DH
    used = jnp.logical_and(lane != 0, lane != DH)

    def halves(v):
        a = jnp.sum(jnp.where(left, v, 0.0), axis=1, keepdims=True)
        b = jnp.sum(jnp.where(left, 0.0, v), axis=1, keepdims=True)
        return jnp.where(left, a, b) * (1.0 / DH)

    def norm(n, top, full):
        n = jnp.where(used, n, 0.0)
        centred = n - halves(n)
        variance = halves(centred * centred)
        scale = jnp.exp(2.0 * (full - top))
        return centred * lax.rsqrt(variance + EPS * scale) * gain_ref[...] + bias_ref[...]

    t0 = norm(n0, top0, full0)
    t1 = norm(n1, top1, full1)
    keys = jnp.where(left, t0, pltpu.roll(t1, DH, 1))
    values = jnp.where(left, pltpu.roll(t0, DH, 1), t1)
    chunk = jnp.concatenate([keys, values], axis=0).astype(bf16)[None]
    out_ref[...] = jnp.broadcast_to(chunk, out_ref.shape)


def far_kernel(group, q2_ref, tab_ref, o_ref, stat_ref, *rest):
    out_ref = rest[-1]
    count = tab_ref.shape[1] // 2
    parts = R // count
    second = stat_ref[HEADS : HEADS + 1, :] > 0.5
    for i, done in enumerate(rest[:-1]):
        out_ref[:, i * LANES : (i + 1) * LANES] = done[...]

    def rows_of(i, part):
        got = tab_ref[i * parts : (i + 1) * parts].astype(f32)
        return got[:, part * count : (part + 1) * count].reshape(R, LANES).astype(bf16)

    def scores_of(i):
        return dot_nt(rows_of(i, 0), q2_ref[group * GROUP + i])

    after = scores_of(0)
    outs = []
    for i in range(GROUP):
        h = group * GROUP + i
        scores = after
        if i + 1 < GROUP:
            after = scores_of(i + 1)
        near_top = stat_ref[h : h + 1, :]
        near_total = stat_ref[2 * HEADS + h : 2 * HEADS + h + 1, :]
        top = jnp.maximum(jnp.max(scores, axis=0, keepdims=True), near_top)
        weight = jnp.exp(scores - top)
        scale = jnp.exp(near_top - top)
        total = jnp.sum(weight, axis=0, keepdims=True) + near_total * scale
        far = dot_tn(rows_of(i, 1), weight.astype(bf16))
        far = jnp.where(second, far[DH:], far[:DH])
        share = 1.0 / total
        outs.append(o_ref[h * DH : (h + 1) * DH] * (scale * share) + far * share)
    for pair in range(GROUP // 2):
        both = jnp.concatenate(outs[2 * pair : 2 * pair + 2], axis=0)
        at = (len(rest) - 1) * GROUP * DH + pair * LANES
        out_ref[:, at : at + LANES] = jnp.transpose(both).astype(bf16)


def on_device(inputs, queries, keys_values, slot_weight, slot_gain, slot_bias, bounds):
    tokens, width = inputs.shape
    shards = lax.axis_size(SEQ)
    shard = lax.axis_index(SEQ)
    split = jnp.where(bounds[0, 0] > 0, bounds[0, 0], bounds[1, 0])
    base = shard * tokens
    yh, c = lax.axis_index("yh"), lax.axis_index("c")
    scal = jnp.stack(
        [
            split - base,
            base,
            jnp.int32(shards * tokens),
            yh * 2 + c,
            yh * 2 + 1 - c,
            (1 - yh) * 2 + c,
            (1 - yh) * 2 + 1 - c,
        ]
    ).astype(jnp.int32)[None]
    x2 = lax.ppermute(inputs, "yh", SWAP)
    x1 = lax.ppermute(inputs, "c", SWAP)
    x3 = lax.ppermute(x2, "c", SWAP)
    up = [(i, i + 1) for i in range(shards - 1)]
    down = [(j, i) for i, j in up]
    before = lax.ppermute(keys_values[:, tokens - W :], SEQ, up)
    after = lax.ppermute(keys_values[:, :W], SEQ, down)

    weight_t = jnp.swapaxes(slot_weight.reshape(4, width, HEADS * R), 1, 2)
    kvh = call(
        prep_kernel,
        jax.ShapeDtypeStruct((HEADS, tokens, 2 * LANES), bf16),
        1, 8, 0, 2 << 20,
    )(scal, keys_values)

    slots = HEADS * R
    flops = 2 * tokens * slots * width
    acc_shape = jax.ShapeDtypeStruct((slots, tokens), f32)
    acc = call(partial_kernel, acc_shape, 3, 16, 2 * flops, 5 << 20)(
        scal, inputs, x1, weight_t
    )
    acc = call(more_kernel, acc_shape, 3, 16, flops, 6 << 20)(scal, x2, weight_t, acc)
    arrived = []
    for g in range(HEADS // GROUP):
        owners = shards
        count = COUNT
        sent = pl.pallas_call(
            functools.partial(project_kernel, g, count),
            out_shape=jax.ShapeDtypeStruct((owners, 2 * count, LANES), bf16),
            in_specs=[VMEM] * 5,
            out_specs=pl.BlockSpec(memory_space=pltpu.HBM),
            scratch_shapes=[
                pltpu.VMEM((GROUP, R // count, 2 * count, LANES), bf16),
                pltpu.SemaphoreType.DMA((GROUP,)),
            ],
            compiler_params=pltpu.CompilerParams(vmem_limit_bytes=16 << 20),
            cost_estimate=pl.CostEstimate(
                flops=flops, bytes_accessed=3 << 20, transcendentals=tokens * slots // 2
            ),
        )(scal, x3, weight_t, acc, kvh)
        arrived.append(lax.all_to_all(sent, ORDER, 0, 0, tiled=True))

    near, stats, q2 = call(
        near_kernel,
        [
            jax.ShapeDtypeStruct((HEADS * DH, tokens), f32),
            jax.ShapeDtypeStruct((4 * HEADS, tokens), f32),
            jax.ShapeDtypeStruct((HEADS, tokens, LANES), bf16),
        ],
        4, 8, 4 * tokens * 3 * W * HEADS * LANES, 2 << 20, tokens * 3 * W * HEADS,
    )(scal, queries, keys_values, before, after)

    outs = []
    size = {name: lax.axis_size(name) for name in SEQ}
    stride = {}
    step = 1
    for name in reversed(SEQ):
        stride[name] = step
        step *= size[name]
    starts = [0]
    for name in ORDER:
        starts = [s + i * stride[name] * tokens for s in starts for i in range(size[name])]
    edge = jnp.int32(0)
    for name in ORDER:
        edge = edge * size[name] + split // tokens // stride[name] % size[name]
    has_edge = split % tokens != 0
    marks = jnp.stack([split, jnp.where(has_edge, edge, 0), has_edge]).astype(jnp.int32)[None]
    head = lax.div(lax.axis_index(ORDER) * COUNT, R)
    gain = lax.dynamic_slice_in_dim(slot_gain, head * DH, DH, 1).reshape(1, 2 * DH)
    bias = lax.dynamic_slice_in_dim(slot_bias, head * DH, DH, 1).reshape(1, 2 * DH)
    chunk = call(
        functools.partial(combine_kernel, starts, tokens),
        jax.ShapeDtypeStruct((shards, 2 * COUNT, LANES), bf16),
        3, 10, 0, 1 << 20, 1 << 17,
        scratch=[pltpu.VMEM((shards, 2 * COUNT, 2 * LANES), f32)],
    )(marks, arrived[0], gain, bias)
    tables = [lax.all_to_all(chunk, ORDER, 0, 0, tiled=True)]

    for g in range(HEADS // GROUP):
        outs.append(
            call(
                functools.partial(far_kernel, g),
                jax.ShapeDtypeStruct((tokens, (g + 1) * GROUP * DH), bf16),
                4 + g, 8, 2 * tokens * R * HEADS * LANES, 1 << 20, tokens * R * GROUP, 0,
            )(q2, tables[g], near, stats, *outs)
        )
    return outs[-1]


def solution(mesh):
    finer = Mesh(mesh.devices.reshape(2, 4, 4, 4, 2, 2), SEQ + DOC)
    return jax.shard_map(
        on_device,
        mesh=finer,
        in_specs=(
            P(SEQ, DOC),
            P(SEQ, DOC),
            P(None, SEQ, DOC),
            P(None, DOC),
            P(None, DOC),
            P(None, DOC),
            P(None, SEQ),
        ),
        out_specs=P(SEQ, DOC),
        check_vma=False,
    )
```
